32 devices in a mesh: dp: 16 (over z, y, x), seq: 2 (over core).
Axes of the slice: x: 2, y: 2, z: 4, core: 2. Of those that a mesh axis runs over, the one named last changes fastest.
Arguments:
- resid: float32 [16, 256, 1024], P('dp', 'seq'), may hold values from -6 to 6
- segment_ids: int32 [16, 256], P('dp'), may hold values from 0 to 2, never falling along the last dimension, each value on 1 to 128 neighbouring positions
- cotangent: float32 [16, 256, 1024], P('dp', 'seq'), may hold values from -6 to 6
- norm_gain: float32 [1024], P(('dp', 'seq')), may hold values from 0.5 to 1.5
- in_weight: float32 [1024, 4384], P(('dp', 'seq')), may hold values from -0.1875 to 0.1875
- conv_weight: float32 [2304, 5], P(('dp', 'seq')), may hold values from -3 to 3
- gate_gain: float32 [2048], P(('dp', 'seq')), may hold values from 0.5 to 1.5
- out_weight: float32 [2048, 1024], P(('dp', 'seq')), may hold values from -0.125 to 0.125
- head_params: float32 [3, 32], replicated, may hold values from -5.4 to 1.5, as said below
- first_norm: float32 [1024], P(('dp', 'seq')), may hold values from -60 to 60
- first_in: float32 [1024, 4384], P(('dp', 'seq')), may hold values from -60 to 60
- first_conv: float32 [2304, 5], P(('dp', 'seq')), may hold values from -60 to 60
- first_gate: float32 [2048], P(('dp', 'seq')), may hold values from -60 to 60
- first_out: float32 [2048, 1024], P(('dp', 'seq')), may hold values from -60 to 60
- first_head: float32 [3, 32], replicated, may hold values from -60 to 60
- second_norm: float32 [1024], P(('dp', 'seq')), may hold values from 10 to 10000
- second_in: float32 [1024, 4384], P(('dp', 'seq')), may hold values from 10 to 10000
- second_conv: float32 [2304, 5], P(('dp', 'seq')), may hold values from 10 to 10000
- second_gate: float32 [2048], P(('dp', 'seq')), may hold values from 10 to 10000
- second_out: float32 [2048, 1024], P(('dp', 'seq')), may hold values from 10 to 10000
- second_head: float32 [3, 32], replicated, may hold values from 10 to 10000
Outputs:
- output: float32 [16, 256, 1024], P('dp', 'seq')
- grad_input: float32 [16, 256, 1024], P('dp', 'seq')
- grad_norm_gain: float32 [1024], P(('dp', 'seq'))
- grad_in_weight: float32 [1024, 4384], P(('dp', 'seq'))
- grad_conv_weight: float32 [2304, 5], P(('dp', 'seq'))
- grad_gate_gain: float32 [2048], P(('dp', 'seq'))
- grad_out_weight: float32 [2048, 1024], P(('dp', 'seq'))
- grad_head_params: float32 [3, 32], replicated
- new_norm_gain: float32 [1024], P(('dp', 'seq'))
- new_in_weight: float32 [1024, 4384], P(('dp', 'seq'))
- new_conv_weight: float32 [2304, 5], P(('dp', 'seq'))
- new_gate_gain: float32 [2048], P(('dp', 'seq'))
- new_out_weight: float32 [2048, 1024], P(('dp', 'seq'))
- new_head_params: float32 [3, 32], replicated
- new_first_norm: float32 [1024], P(('dp', 'seq'))
- new_first_in: float32 [1024, 4384], P(('dp', 'seq'))
- new_first_conv: float32 [2304, 5], P(('dp', 'seq'))
- new_first_gate: float32 [2048], P(('dp', 'seq'))
- new_first_out: float32 [2048, 1024], P(('dp', 'seq'))
- new_first_head: float32 [3, 32], replicated
- new_second_norm: float32 [1024], P(('dp', 'seq'))
- new_second_in: float32 [1024, 4384], P(('dp', 'seq'))
- new_second_conv: float32 [2304, 5], P(('dp', 'seq'))
- new_second_gate: float32 [2048], P(('dp', 'seq'))
- new_second_out: float32 [2048, 1024], P(('dp', 'seq'))
- new_second_head: float32 [3, 32], replicated
The draws below stay inside these ranges and needn't reach their ends.
Inputs may be any that keep to these rules, and one draw needn't show every extreme that they name: `segment_ids`: segment numbers never fall along a sequence, start at 0 and rise by one at each document boundary; each document holds 1 to 128 tokens. `head_params`: row 0 holds log decay rates, row 1 step biases, row 2 skip gains.
All inputs are finite; a program needn't handle non-finite values.
Results may differ from the reference program's by a relative error of at most 0.012.
Values may be sent and summed in bfloat16 or wider, within the bound.
No kernel may reach another device: no remote copies, remote signals or barrier semaphores. Data moves between devices by JAX's collectives and lax.ppermute only.
A program may use at most 128 MiB of HBM per device.

```python
import math
import jax
import jax.numpy as jnp
import numpy as np
from jax import lax

D = 1024
H = 32
P_SIZE = 64
N = 128
CK = 4
BLOCK = 128
STEP = 4
DI = 2048
CONV = 2304
E = 4384
SEQ_LEN = 256
SEQS = 16


def draw_head_params(key, part):
    subkeys = jax.random.split(jax.random.fold_in(key, 17), 3)
    log_rate = jax.random.uniform(subkeys[0], (H,), jnp.float32, math.log(0.0045), math.log(1.0))
    step_bias = jax.random.uniform(subkeys[1], (H,), jnp.float32, -4.0, -2.5)
    skip_gain = jax.random.uniform(subkeys[2], (H,), jnp.float32, 0.5, 1.5)
    return jnp.stack([log_rate, step_bias, skip_gain])


def shard_levels(own_key, extent, cuts, smallest, high):
    def one(axis_at, shards_of):
        steps = jax.random.uniform(jax.random.fold_in(jax.random.fold_in(own_key, 6), axis_at), (shards_of,), jnp.float32, smallest / len(cuts), high / len(cuts))
        return jnp.repeat(jnp.exp(steps), extent[axis_at] // shards_of).reshape((-1,) + (1,) * (len(extent) - axis_at - 1))

    factor_of = one(*cuts[0])
    for cut in cuts[1:]:
        factor_of = factor_of * one(*cut)
    return factor_of


def profile(number_of, total, bound, skew):
    portions = [(1 << 20) // math.isqrt(grade ** skew) + 1 for grade in range(2, number_of + 1)]
    surplus, given = total - bound - (number_of - 1), [1] * (number_of - 1)
    while surplus > 0:
        movable = [i for i in range(number_of - 1) if given[i] < bound]
        whole, budget = sum([portions[i] for i in movable]), surplus
        for i in movable:
            addition = min(bound - given[i], max(1, budget * portions[i] // whole), surplus)
            given[i] = given[i] + addition
            surplus = surplus - addition
    return np.array([bound] + given)


def uneven_parts(stream_key, number_of, total, most, lean):
    if number_of == 2:
        one = jax.random.randint(stream_key, (), max(1, total - most), min(most, total - 1) + 1)
        return jnp.stack([one, total - one])
    tallies = jnp.asarray(profile(number_of, total, most, lean), jnp.int32)
    couples = (number_of - 1) // 2
    donor, sink = tallies[1:1 + 2 * couples:2], tallies[2:2 + 2 * couples:2]
    slack = jnp.minimum(donor - 1, most - sink)
    passed = jax.random.randint(jax.random.fold_in(stream_key, 1), (couples,), 0, 1 << 20) % (slack + 1)
    tallies = tallies.at[1:1 + 2 * couples:2].set(donor - passed).at[2:2 + 2 * couples:2].set(sink + passed)
    return tallies[jax.random.permutation(jax.random.fold_in(stream_key, 2), number_of)]


def scatter_about(own_key, extent, scale, bound, cuts=(), held_as=jnp.bfloat16):
    factor_of = shard_levels(own_key, extent, cuts, -0.22, 0.18) if cuts else 1.0
    drawn = jax.random.normal(own_key, extent, jnp.float32) * scale * factor_of
    return jnp.minimum(jnp.maximum(drawn, -bound), bound).astype(held_as)


def setup_inputs(seed: int = 0) -> dict:
    key_list = jax.random.split(jax.random.key(seed), 22)
    return {
        "resid": scatter_about(key_list[0], (SEQS, SEQ_LEN, D), 1.0, 6.0, ((0, 16), (1, 2)), jnp.float32),
        "segment_ids": jax.vmap(lambda own: jnp.searchsorted(jnp.cumsum(uneven_parts(own, 3, SEQ_LEN, SEQ_LEN // 2, 0)), jnp.arange(SEQ_LEN), side="right"))(jax.random.split(key_list[1], SEQS)).reshape((SEQS, SEQ_LEN)).astype(jnp.int32),
        "cotangent": scatter_about(key_list[2], (SEQS, SEQ_LEN, D), 1.0, 6.0, ((0, 16), (1, 2)), jnp.float32),
        "norm_gain": jnp.clip(1.0 + 0.1 * jax.random.normal(key_list[3], (D,), jnp.float32), 0.5, 1.5),
        "in_weight": scatter_about(key_list[4], (D, E), D ** -0.5, 0.1875, ((0, 32),), jnp.float32),
        "conv_weight": scatter_about(key_list[5], (CONV, CK + 1), CK ** -0.5, 3.0, ((0, 32),), jnp.float32),
        "gate_gain": jnp.clip(1.0 + 0.1 * jax.random.normal(key_list[6], (DI,), jnp.float32), 0.5, 1.5),
        "out_weight": scatter_about(key_list[7], (DI, D), DI ** -0.5, 0.125, ((0, 32),), jnp.float32),
        "head_params": draw_head_params(jax.random.fold_in(key_list[21], 71), 0),
        "first_norm": scatter_about(key_list[9], (D,), 10.0, 60.0, ((0, 32),), jnp.float32),
        "first_in": scatter_about(key_list[10], (D, E), 10.0, 60.0, ((0, 32),), jnp.float32),
        "first_conv": scatter_about(key_list[11], (CONV, CK + 1), 10.0, 60.0, ((0, 32),), jnp.float32),
        "first_gate": scatter_about(key_list[12], (DI,), 10.0, 60.0, ((0, 32),), jnp.float32),
        "first_out": scatter_about(key_list[13], (DI, D), 10.0, 60.0, ((0, 32),), jnp.float32),
        "first_head": scatter_about(key_list[14], (3, H), 10.0, 60.0, (), jnp.float32),
        "second_norm": jnp.clip(jnp.exp(math.log(10000.0) - 6.9077553 * jax.random.uniform(key_list[15], (D,), jnp.float32) ** shard_levels(key_list[15], (D,), ((0, 32),), -0.2, 0.2)), 10.0, 10000.0),
        "second_in": jnp.clip(jnp.exp(math.log(10000.0) - 6.9077553 * jax.random.uniform(key_list[16], (D, E), jnp.float32) ** shard_levels(key_list[16], (D, E), ((0, 32),), -0.2, 0.2)), 10.0, 10000.0),
        "second_conv": jnp.clip(jnp.exp(math.log(10000.0) - 6.9077553 * jax.random.uniform(key_list[17], (CONV, CK + 1), jnp.float32) ** shard_levels(key_list[17], (CONV, CK + 1), ((0, 32),), -0.2, 0.2)), 10.0, 10000.0),
        "second_gate": jnp.clip(jnp.exp(math.log(10000.0) - 6.9077553 * jax.random.uniform(key_list[18], (DI,), jnp.float32) ** shard_levels(key_list[18], (DI,), ((0, 32),), -0.2, 0.2)), 10.0, 10000.0),
        "second_out": jnp.clip(jnp.exp(math.log(10000.0) - 6.9077553 * jax.random.uniform(key_list[19], (DI, D), jnp.float32) ** shard_levels(key_list[19], (DI, D), ((0, 32),), -0.2, 0.2)), 10.0, 10000.0),
        "second_head": jnp.clip(jnp.exp(jax.random.uniform(key_list[20], (3, H), jnp.float32, math.log(10.0), math.log(10000.0))), 10.0, 10000.0),
    }


NORM_EPS = 1e-05
LEARNING_RATE = 0.02
BETA_FIRST = 0.9
BETA_SECOND = 0.95
ADAM_EPS = 1e-08
WEIGHT_DECAY = 0.1
HIGHEST = lax.Precision.HIGHEST
MASKED = -1e+30

def rms_scale(values, gain):
    return values * lax.rsqrt(lax.optimization_barrier(jnp.mean(values * values, axis=-1, keepdims=True)) + NORM_EPS) * gain

def prepare(projected, edge_rows, segments, seg_edge, conv_taps, head_params):
    length = projected.shape[0]
    heads = head_params.shape[1]
    inner = heads * P_SIZE
    width = conv_taps.shape[0]
    conv_input = projected[:, inner:inner + width]
    padded = jnp.concatenate([edge_rows, conv_input], axis=0)
    padded_segs = jnp.concatenate([seg_edge, segments])
    mixed_conv = jnp.zeros_like(conv_input) + conv_taps[:, CK][None, :]
    for offset in range(CK):
        window = padded[offset:offset + length]
        same_doc = (padded_segs[offset:offset + length] == segments).astype(jnp.float32)
        mixed_conv = mixed_conv + conv_taps[:, offset][None, :] * window * same_doc[:, None]
    activated = jax.nn.silu(mixed_conv)
    head_inputs = activated[:, :inner].reshape(length, heads, P_SIZE)
    write_rows = activated[:, inner:inner + N]
    read_rows = activated[:, inner + N:]
    timestep = jax.nn.softplus(projected[:, inner + width:] + head_params[1][None, :])
    decay_rate = -jnp.exp(head_params[0])[None, :] * timestep
    return (head_inputs, write_rows, read_rows, timestep, decay_rate)

def block_step(head_inputs, write_rows, read_rows, timestep, decay_rate, segments, prior_seg, ssm_state, with_output):
    cumulative = jnp.cumsum(decay_rate, axis=0)
    summed = cumulative[-1]
    tail_mask = (segments == segments[-1]).astype(jnp.float32)
    carry_on = (segments[-1] == prior_seg).astype(jnp.float32)
    tail_weight = jnp.exp(summed[None, :] - cumulative) * timestep * tail_mask[:, None]
    new_state = jnp.einsum('shp,sn->hpn', head_inputs * tail_weight[:, :, None], write_rows, precision=HIGHEST)
    new_state = new_state + (jnp.exp(summed) * carry_on)[:, None, None] * ssm_state
    if not with_output:
        return (None, new_state)
    length = segments.shape[0]
    positions = jnp.arange(length)
    visible = (segments[:, None] == segments[None, :]) & (positions[:, None] >= positions[None, :])
    spread = cumulative.T[:, :, None] - cumulative.T[:, None, :]
    affinity = jnp.dot(read_rows, write_rows.T, precision=HIGHEST)
    scores = affinity[None] * jnp.exp(jnp.where(visible[None], spread, MASKED))
    output = jnp.einsum('hts,shp->thp', scores, head_inputs * timestep[:, :, None], precision=HIGHEST)
    entry_weight = jnp.exp(cumulative) * (segments == prior_seg).astype(jnp.float32)[:, None]
    output = output + jnp.einsum('tn,hpn->thp', read_rows, ssm_state, precision=HIGHEST) * entry_weight[:, :, None]
    return (output, new_state)

def run_blocks(head_inputs, write_rows, read_rows, timestep, decay_rate, segments, prior_seg, ssm_state, with_output):
    block_count = segments.shape[0] // BLOCK

    def blocked(values):
        return values.reshape((block_count, BLOCK) + values.shape[1:])

    def advance(carried, pieces):
        output, new_state = block_step(*pieces, carried[1], carried[0], with_output)
        return ((new_state, pieces[5][-1]), output)
    inputs = tuple((blocked(values) for values in (head_inputs, write_rows, read_rows, timestep, decay_rate, segments)))
    (final_state, _), outputs = lax.scan(advance, (ssm_state, prior_seg), inputs)
    if with_output:
        outputs = outputs.reshape((segments.shape[0],) + outputs.shape[2:])
    return (outputs, final_state)

def scan_gated(projected, edge_rows, ssm_state, conv_taps, head_params, segments, seg_edge):
    head_inputs, write_rows, read_rows, timestep, decay_rate = prepare(projected, edge_rows, segments, seg_edge, conv_taps, head_params)
    output, final_state = run_blocks(head_inputs, write_rows, read_rows, timestep, decay_rate, segments, seg_edge[-1], ssm_state, True)
    output = output + head_params[2][None, :, None] * head_inputs
    inner = head_inputs.shape[1] * P_SIZE
    gated = output.reshape(projected.shape[0], inner) * jax.nn.silu(projected[:, :inner])
    return (gated, final_state)

def adamw(weight, gradient, first_moment, second_moment):
    first_new = BETA_FIRST * first_moment + (1.0 - BETA_FIRST) * gradient
    second_new = BETA_SECOND * second_moment + (1.0 - BETA_SECOND) * gradient * gradient
    first_hat = first_new / (1.0 - BETA_FIRST ** STEP)
    second_hat = second_new / (1.0 - BETA_SECOND ** STEP)
    weight_new = weight - LEARNING_RATE * (first_hat / (jnp.sqrt(second_hat) + ADAM_EPS) + WEIGHT_DECAY * weight)
    return (weight_new, first_new, second_new)

def reference(resid, segment_ids, cotangent, norm_gain, in_weight, conv_weight, gate_gain, out_weight, head_params, first_norm, first_in, first_conv, first_gate, first_out, first_head, second_norm, second_in, second_conv, second_gate, second_out, second_head):
    in_copy = in_weight.astype(jnp.bfloat16)
    out_copy = out_weight.astype(jnp.bfloat16)
    norm_wide = norm_gain.astype(jnp.bfloat16).astype(jnp.float32)
    conv_wide = conv_weight.astype(jnp.bfloat16).astype(jnp.float32)
    gate_wide = gate_gain.astype(jnp.bfloat16).astype(jnp.float32)
    contract_rows = (((0,), (0,)), ((), ()))
    contract_cols = (((1,), (1,)), ((), ()))

    def per_sequence(totals, inputs):
        local_rows, segments, cot_rows = inputs
        normed = rms_scale(local_rows, norm_wide)
        normed_half = normed.astype(jnp.bfloat16)
        projected = jnp.dot(normed_half, in_copy, preferred_element_type=jnp.float32)
        edge_rows = jnp.zeros((CK - 1, CONV), jnp.float32)
        seg_edge = jnp.full((CK - 1,), segments[0], jnp.int32)
        empty_state = jnp.zeros((H, P_SIZE, N), jnp.float32)

        def local_mix(projected, conv_taps, gate_scale, head_params):
            gated = scan_gated(projected, edge_rows, empty_state, conv_taps, head_params, segments, seg_edge)[0]
            return rms_scale(gated, gate_scale)
        mixed_rows, pullback = jax.vjp(local_mix, projected, conv_wide, gate_wide, head_params)
        mixed_half = mixed_rows.astype(jnp.bfloat16)
        result = local_rows + jnp.dot(mixed_half, out_copy, preferred_element_type=jnp.float32)
        cot_half = cot_rows.astype(jnp.bfloat16)
        grad_out_w = lax.dot_general(mixed_half, cot_half, contract_rows, preferred_element_type=jnp.float32)
        grad_mixed = lax.dot_general(cot_half, out_copy, contract_cols, preferred_element_type=jnp.float32)
        grad_proj, grad_conv, grad_gate, grad_head = pullback(grad_mixed)
        grad_proj_half = grad_proj.astype(jnp.bfloat16)
        grad_in_w = lax.dot_general(normed_half, grad_proj_half, contract_rows, preferred_element_type=jnp.float32)
        grad_normed = lax.dot_general(grad_proj_half, in_copy, contract_cols, preferred_element_type=jnp.float32)
        _, norm_pull = jax.vjp(rms_scale, local_rows, norm_wide)
        grad_rows, grad_norm = norm_pull(grad_normed)
        totals = (totals[0] + grad_norm, totals[1] + grad_in_w, totals[2] + grad_conv, totals[3] + grad_gate, totals[4] + grad_out_w, totals[5] + grad_head)
        return (totals, (result, cot_rows + grad_rows))
    starting = (jnp.zeros((D,), jnp.float32), jnp.zeros((D, E), jnp.float32), jnp.zeros((CONV, CK + 1), jnp.float32), jnp.zeros((DI,), jnp.float32), jnp.zeros((DI, D), jnp.float32), jnp.zeros((3, H), jnp.float32))
    totals, (output, grad_input) = lax.scan(per_sequence, starting, (resid, segment_ids, cotangent))
    new_norm, new_first_norm, new_second_norm = adamw(norm_gain, totals[0], first_norm, second_norm)
    new_in, new_first_in, new_second_in = adamw(in_weight, totals[1], first_in, second_in)
    new_conv, new_first_conv, new_second_conv = adamw(conv_weight, totals[2], first_conv, second_conv)
    new_gate, new_first_gate, new_second_gate = adamw(gate_gain, totals[3], first_gate, second_gate)
    new_out, new_first_out, new_second_out = adamw(out_weight, totals[4], first_out, second_out)
    new_head, new_first_head, new_second_head = adamw(head_params, totals[5], first_head, second_head)
    return (output, grad_input, totals[0], totals[1], totals[2], totals[3], totals[4], totals[5], new_norm, new_in, new_conv, new_gate, new_out, new_head, new_first_norm, new_first_in, new_first_conv, new_first_gate, new_first_out, new_first_head, new_second_norm, new_second_in, new_second_conv, new_second_gate, new_second_out, new_second_head)
```

```python
import functools

import jax
import jax.numpy as jnp
from jax import lax
from jax.experimental import pallas as pl
from jax.experimental.pallas import tpu as pltpu
from jax.sharding import PartitionSpec as P

H = 32
P_SIZE = 64
N = 128
CK = 4
BLOCK = 128
STEP = 4
DI = 2048
CONV = 2304


NORM_EPS = 1e-05
LEARNING_RATE = 0.02
BETA_FIRST = 0.9
BETA_SECOND = 0.95
ADAM_EPS = 1e-08
WEIGHT_DECAY = 0.1
HIGHEST = lax.Precision.HIGHEST
MASKED = -1e30
INTERPRET = False

PLANES = 2
HP = H // PLANES
IP = HP * P_SIZE
CP = IP + 2 * N
PAIR = 2 * P_SIZE
SMALL = CP + HP
WA = -(-(SMALL + 24) // 128) * 128
LOW = jnp.bfloat16
F32 = jnp.float32
ROWS_COLS = (((0,), (0,)), ((), ()))
COLS_COLS = (((1,), (1,)), ((), ()))


def mm(a, b, dims=(((1,), (0,)), ((), ()))):
    return lax.dot_general(a.astype(LOW), b.astype(LOW), dims, preferred_element_type=F32)


def exact_mm(a, b, dims=(((1,), (0,)), ((), ()))):
    return lax.dot_general(a, b, dims, precision=HIGHEST, preferred_element_type=F32)


def sibling(x):
    return lax.ppermute(x, "seq", [(0, 1), (1, 0)])


def both_halves(x):
    other = sibling(x)
    first = lax.axis_index("seq") == 0
    return jnp.concatenate([jnp.where(first, x, other), jnp.where(first, other, x)], axis=0)


def own_half(x):
    half = x.shape[0] // 2
    first = lax.axis_index("seq") == 0
    low, high = x[:half], x[half:]
    return jnp.where(first, low, high) + sibling(jnp.where(first, high, low))


def planes_of(x, axis):
    shape = x.shape
    width = shape[axis] // H
    split = x.reshape(shape[:axis] + (HP, PLANES, width) + shape[axis + 1 :])
    return [
        lax.index_in_dim(split, p, axis + 1, keepdims=False).reshape(
            shape[:axis] + (HP * width,) + shape[axis + 1 :]
        )
        for p in range(PLANES)
    ]


def interleave(even, odd, axis):
    shape = even.shape
    width = shape[axis] // HP
    parts = [
        v.reshape(shape[:axis] + (HP, 1, width) + shape[axis + 1 :]) for v in (even, odd)
    ]
    return jnp.concatenate(parts, axis=axis + 1).reshape(
        shape[:axis] + (H * width,) + shape[axis + 1 :]
    )


def adamw(weight, gradient, first_moment, second_moment):
    first_new = BETA_FIRST * first_moment + (1.0 - BETA_FIRST) * gradient
    second_new = BETA_SECOND * second_moment + (1.0 - BETA_SECOND) * gradient * gradient
    first_hat = first_new / (1.0 - BETA_FIRST**STEP)
    second_hat = second_new / (1.0 - BETA_SECOND**STEP)
    weight_new = weight - LEARNING_RATE * (
        first_hat / (jnp.sqrt(second_hat) + ADAM_EPS) + WEIGHT_DECAY * weight
    )
    return (weight_new, first_new, second_new)


def sigmoid(v):
    return 1.0 / (1.0 + jnp.exp(-v))


def softplus(v):
    return jnp.maximum(v, 0.0) + jnp.log1p(jnp.exp(-jnp.abs(v)))


def lower_ones(length):
    row = lax.broadcasted_iota(jnp.int32, (length, length), 0)
    col = lax.broadcasted_iota(jnp.int32, (length, length), 1)
    return (row >= col).astype(F32)


def column(values, index):
    return values[:, index : index + 1]


def per_pair(values, pair, lanes_low):
    return jnp.where(lanes_low, column(values, 2 * pair), column(values, 2 * pair + 1))


def steps_of(dt_raw, heads):
    raw = dt_raw + heads[1:2, :]
    timestep = softplus(raw)
    decay = -jnp.exp(heads[0:1, :]) * timestep
    return raw, timestep, decay


def block_sums(decay):
    ones = lower_ones(BLOCK)
    columns, rows = [], []
    for b in range(decay.shape[0] // BLOCK):
        part = decay[b * BLOCK : (b + 1) * BLOCK]
        columns.append(exact_mm(ones, part))
        rows.append(exact_mm(part, ones, (((0,), (1,)), ((), ()))))
    return columns, rows


def visible_in(seg_col, seg_row, b):
    span = slice(b * BLOCK, (b + 1) * BLOCK)
    row = lax.broadcasted_iota(jnp.int32, (BLOCK, BLOCK), 0)
    col = lax.broadcasted_iota(jnp.int32, (BLOCK, BLOCK), 1)
    return (seg_col[span] == seg_row[:, span]) & (row >= col)


def across(seg_col, seg_row, b):
    return seg_col[b * BLOCK : (b + 1) * BLOCK] == seg_row[:, (b - 1) * BLOCK : b * BLOCK]


def forward_kernel(proj_ref, taps_ref, heads_ref, segc_ref, segr_ref, mask_ref, pre_ref, y_ref):
    tokens = proj_ref.shape[0]
    blocks = tokens // BLOCK
    heads = heads_ref[...]
    seg_col, seg_row = segc_ref[...], segr_ref[...]
    mask = mask_ref[...]
    taps = taps_ref[...]

    def convolve(lanes):
        source = proj_ref[:, lanes]
        total = taps[CK : CK + 1, lanes] + taps[CK - 1 : CK, lanes] * source
        for back in range(1, CK):
            moved = pltpu.roll(source, back, 0) * column(mask, back)
            total = total + taps[CK - 1 - back : CK - back, lanes] * moved
        pre_ref[:, lanes] = total
        return total * sigmoid(total)

    write_rows = convolve(slice(IP, IP + N))
    read_rows = convolve(slice(IP + N, CP))
    _, timestep, decay = steps_of(proj_ref[:, CP : CP + HP], heads)
    sums_col, sums_row = block_sums(decay)
    affinity, crossing = [], [None]
    for b in range(blocks):
        span = slice(b * BLOCK, (b + 1) * BLOCK)
        affinity.append(mm(read_rows[span], write_rows[span], COLS_COLS))
        if b:
            before = slice((b - 1) * BLOCK, b * BLOCK)
            crossing.append(
                jnp.where(
                    across(seg_col, seg_row, b), mm(read_rows[span], write_rows[before], COLS_COLS), 0.0
                ).astype(LOW)
            )
    seen = [visible_in(seg_col, seg_row, b) for b in range(blocks)]
    lanes_low = lax.broadcasted_iota(jnp.int32, (1, PAIR), 1) < P_SIZE
    entry = [jnp.exp(c) for c in sums_col]
    tail = [jnp.exp(c[BLOCK - 1 : BLOCK, :] - c) for c in sums_col]
    for pair in range(HP // 2):
        lanes = slice(pair * PAIR, (pair + 1) * PAIR)
        inputs = convolve(lanes)
        scaled = inputs * per_pair(timestep, pair, lanes_low)
        skip = jnp.where(lanes_low, heads[2:3, 2 * pair : 2 * pair + 1], heads[2:3, 2 * pair + 1 : 2 * pair + 2])
        for b in range(blocks):
            span = slice(b * BLOCK, (b + 1) * BLOCK)
            scores = []
            for h in (2 * pair, 2 * pair + 1):
                spread = column(sums_col[b], h) - sums_row[b][h : h + 1, :]
                scores.append((affinity[b] * jnp.exp(jnp.where(seen[b], spread, MASKED))).astype(LOW))
            here = scaled[span]
            stacked = jnp.concatenate(
                [jnp.where(lanes_low, here, 0.0), jnp.where(lanes_low, 0.0, here)], axis=0
            )
            out = mm(jnp.concatenate(scores, axis=1), stacked)
            if b:
                before = slice((b - 1) * BLOCK, b * BLOCK)
                weighted = scaled[before] * per_pair(tail[b - 1], pair, lanes_low)
                out = out + per_pair(entry[b], pair, lanes_low) * mm(crossing[b], weighted)
            y_ref[span, lanes] = out + skip * inputs[span]


def backward_kernel(
    proj_ref,
    z_ref,
    pre_ref,
    y_ref,
    gm_ref,
    sums_ref,
    gate_ref,
    taps_ref,
    heads_ref,
    segc_ref,
    segr_ref,
    mask_ref,
    da_ref,
    dz_ref,
    dtaps_ref,
    dgate_ref,
    dheads_ref,
):
    tokens = proj_ref.shape[0]
    blocks = tokens // BLOCK
    heads = heads_ref[...]
    seg_col, seg_row = segc_ref[...], segr_ref[...]
    mask = mask_ref[...]
    taps = taps_ref[...]
    scale = sums_ref[:, 0:1]
    pull = sums_ref[:, 1:2]

    def activate(lanes):
        pre = pre_ref[:, lanes]
        sig = sigmoid(pre)
        return pre * sig, sig * (1.0 + pre * (1.0 - sig))

    def unconvolve(lanes, grad):
        source = proj_ref[:, lanes]
        result = taps[CK - 1 : CK, lanes] * grad
        dtaps_ref[CK : CK + 1, lanes] = jnp.sum(grad, axis=0, keepdims=True)
        dtaps_ref[CK - 1 : CK, lanes] = jnp.sum(grad * source, axis=0, keepdims=True)
        for back in range(1, CK):
            at = CK - 1 - back
            kept = grad * column(mask, back)
            moved = pltpu.roll(kept, tokens - back, 0)
            dtaps_ref[at : at + 1, lanes] = jnp.sum(moved * source, axis=0, keepdims=True)
            result = result + taps[at : at + 1, lanes] * moved
        da_ref[:, lanes] = result.astype(LOW)

    write_rows, write_slope = activate(slice(IP, IP + N))
    read_rows, read_slope = activate(slice(IP + N, CP))
    raw, timestep, decay = steps_of(proj_ref[:, CP : CP + HP], heads)
    sums_col, sums_row = block_sums(decay)
    affinity, crossing = [], [None]
    for b in range(blocks):
        span = slice(b * BLOCK, (b + 1) * BLOCK)
        affinity.append(mm(read_rows[span], write_rows[span], COLS_COLS))
        if b:
            before = slice((b - 1) * BLOCK, b * BLOCK)
            crossing.append(
                jnp.where(
                    across(seg_col, seg_row, b), mm(read_rows[span], write_rows[before], COLS_COLS), 0.0
                ).astype(LOW)
            )
    seen = [visible_in(seg_col, seg_row, b) for b in range(blocks)]
    lanes_low = lax.broadcasted_iota(jnp.int32, (1, PAIR), 1) < P_SIZE
    head_lane = lax.broadcasted_iota(jnp.int32, (1, HP), 1)
    entry = [jnp.exp(c) for c in sums_col]
    tail = [jnp.exp(c[BLOCK - 1 : BLOCK, :] - c) for c in sums_col]
    d_affinity = [jnp.zeros((BLOCK, BLOCK), F32) for _ in range(blocks)]
    d_crossing = [jnp.zeros((BLOCK, BLOCK), F32) for _ in range(blocks)]
    d_sums = [jnp.zeros((BLOCK, HP), F32) for _ in range(blocks)]
    d_steps = [jnp.zeros((BLOCK, HP), F32) for _ in range(blocks)]
    d_skip = jnp.zeros((1, HP), F32)

    def spread_heads(values, pair):
        low = jnp.sum(jnp.where(lanes_low, values, 0.0), axis=1, keepdims=True)
        high = jnp.sum(jnp.where(lanes_low, 0.0, values), axis=1, keepdims=True)
        return jnp.where(head_lane == 2 * pair, low, 0.0) + jnp.where(
            head_lane == 2 * pair + 1, high, 0.0
        )

    for pair in range(HP // 2):
        lanes = slice(pair * PAIR, (pair + 1) * PAIR)
        inputs, slope = activate(lanes)
        step = per_pair(timestep, pair, lanes_low)
        scaled = inputs * step
        skip = jnp.where(lanes_low, heads[2:3, 2 * pair : 2 * pair + 1], heads[2:3, 2 * pair + 1 : 2 * pair + 2])
        z = z_ref[:, lanes]
        sig = sigmoid(z)
        silu = z * sig
        y = y_ref[:, lanes]
        gated = y * silu
        gm = gm_ref[:, lanes]
        dgate_ref[:, lanes] = jnp.sum(gm * gated * scale, axis=0, keepdims=True)
        d_gated = scale * (gm * gate_ref[:, lanes]) - gated * pull
        dz_ref[:, lanes] = (d_gated * y * (sig * (1.0 + z * (1.0 - sig)))).astype(LOW)
        d_y = d_gated * silu
        d_skip = d_skip + jnp.sum(spread_heads(d_y * inputs, pair), axis=0, keepdims=True)
        d_y_low = d_y.astype(LOW)
        d_y_round = d_y_low.astype(F32)
        scan = y - skip * inputs
        scaled_low = scaled.astype(LOW)
        scaled_round = scaled_low.astype(F32)
        d_scaled = [None] * blocks
        for b in range(blocks):
            span = slice(b * BLOCK, (b + 1) * BLOCK)
            grads, here = d_y_round[span], scaled_low[span]
            stacked = jnp.concatenate(
                [jnp.where(lanes_low, grads, 0.0), jnp.where(lanes_low, 0.0, grads)], axis=0
            ).astype(LOW)
            d_scores = mm(stacked, here, COLS_COLS)
            scores = []
            for i, h in enumerate((2 * pair, 2 * pair + 1)):
                spread = column(sums_col[b], h) - sums_row[b][h : h + 1, :]
                fade = jnp.exp(jnp.where(seen[b], spread, MASKED))
                d_affinity[b] = d_affinity[b] + d_scores[i * BLOCK : (i + 1) * BLOCK] * fade
                scores.append((affinity[b] * fade).astype(LOW))
            d_here = mm(jnp.concatenate(scores, axis=0), stacked, ROWS_COLS)
            d_scaled[b] = d_here if d_scaled[b] is None else d_scaled[b] + d_here
            d_sums[b] = d_sums[b] + spread_heads(grads * scan[span], pair)
            if b:
                before = slice((b - 1) * BLOCK, b * BLOCK)
                tail_here = per_pair(tail[b - 1], pair, lanes_low)
                weighted = (scaled[before] * tail_here).astype(LOW)
                incoming = (d_y[span] * per_pair(entry[b], pair, lanes_low)).astype(LOW)
                d_weighted = mm(crossing[b], incoming, ROWS_COLS)
                d_crossing[b] = d_crossing[b] + mm(incoming, weighted, COLS_COLS)
                d_scaled[b - 1] = d_scaled[b - 1] + tail_here * d_weighted
        for b in range(blocks):
            span = slice(b * BLOCK, (b + 1) * BLOCK)
            d_sums[b] = d_sums[b] - spread_heads(scaled_round[span] * d_scaled[b], pair)
            d_steps[b] = d_steps[b] + spread_heads(inputs[span] * d_scaled[b], pair)
        d_inputs = jnp.concatenate(d_scaled, axis=0) * step + skip * d_y
        unconvolve(lanes, d_inputs * slope)

    ones = lower_ones(BLOCK)
    d_write = [jnp.zeros((BLOCK, N), F32) for _ in range(blocks)]
    d_read = [None] * blocks
    d_decay = [None] * blocks
    later = jnp.zeros((1, HP), F32)
    for b in range(blocks):
        span = slice(b * BLOCK, (b + 1) * BLOCK)
        d_read[b] = mm(d_affinity[b], write_rows[span])
        d_write[b] = d_write[b] + mm(d_affinity[b], read_rows[span], ROWS_COLS)
        if b:
            before = slice((b - 1) * BLOCK, b * BLOCK)
            kept = jnp.where(across(seg_col, seg_row, b), d_crossing[b], 0.0)
            d_read[b] = d_read[b] + mm(kept, write_rows[before])
            d_write[b - 1] = d_write[b - 1] + mm(kept, read_rows[span], ROWS_COLS)
    for b in reversed(range(blocks)):
        d_decay[b] = exact_mm(ones, d_sums[b], ROWS_COLS) + later
        later = later + jnp.sum(d_sums[b], axis=0, keepdims=True)
    unconvolve(slice(IP, IP + N), jnp.concatenate(d_write, axis=0) * write_slope)
    unconvolve(slice(IP + N, CP), jnp.concatenate(d_read, axis=0) * read_slope)
    d_decay = jnp.concatenate(d_decay, axis=0)
    d_raw = (jnp.concatenate(d_steps, axis=0) - d_decay * jnp.exp(heads[0:1, :])) * sigmoid(raw)
    padding = jnp.zeros((tokens, WA - SMALL), LOW)
    da_ref[:, CP:WA] = jnp.concatenate([d_raw.astype(LOW), padding], axis=1)
    dheads_ref[0:1, :] = jnp.sum(d_decay * decay, axis=0, keepdims=True)
    dheads_ref[1:2, :] = jnp.sum(d_raw, axis=0, keepdims=True)
    dheads_ref[2:3, :] = d_skip


def call(kernel, outs, *args):
    return pl.pallas_call(
        kernel,
        out_shape=[jax.ShapeDtypeStruct(shape, kind) for shape, kind in outs],
        interpret=INTERPRET,
    )(*args)


def gather(x):
    return lax.all_gather(x, "dp", axis=0, tiled=True)


def scatter(x):
    return lax.psum_scatter(x, "dp", scatter_dimension=0, tiled=True)


def small_width(rows):
    per_core = CONV // (DI // P_SIZE)
    return per_core * (CK + 1), -(-(per_core * (CK + 1)) // rows)


def fetch(norm_low, in_low, conv_low, gate_low, out_low):
    place = lax.axis_index("seq")
    rows = in_low.shape[0]
    values, width = small_width(rows)
    z = planes_of(in_low[:, :DI], 1)
    x = planes_of(in_low[:, DI : 2 * DI], 1)
    shared = in_low[:, 2 * DI : DI + CONV]
    steps = planes_of(in_low[:, DI + CONV :], 1)
    conv_flat = jnp.pad(conv_low.reshape(-1), (0, rows * width - values)).reshape(rows, width)
    gate_two = gate_low.reshape(2, rows).T
    payload = []
    for p in range(PLANES):
        gate_here = jnp.where(place == p, gate_two, jnp.zeros_like(gate_two))
        pieces = [x[p], shared, steps[p], norm_low[:, None], gate_here, conv_flat]
        used = SMALL + 3 + width
        pieces.append(jnp.zeros((rows, WA - used), LOW))
        pieces.append(z[p])
        payload.append(jnp.concatenate(pieces, axis=1))
    first = place == 0
    mine = jnp.where(first, payload[0], payload[1])
    other = sibling(jnp.where(first, payload[1], payload[0]))
    chip = jnp.concatenate([jnp.where(first, mine, other), jnp.where(first, other, mine)], axis=0)
    w_a = gather(chip[:, :WA])
    w_z = gather(chip[:, WA:])
    w_out = gather(out_low)
    chips = w_a.shape[0] // (2 * rows)
    small = w_a[:, SMALL : SMALL + 3 + width].astype(F32)
    norm = small[:, 0]
    gate = small[:, 1:3].reshape(chips, 2, rows, 2).sum(1).transpose(0, 2, 1).reshape(-1)
    conv = small[:, 3:].reshape(2 * chips, rows * width)[:, :values].reshape(CONV, CK + 1).T
    return w_a, w_z, w_out, norm, gate, plane_taps(conv)


def plane_taps(conv):
    x = planes_of(conv[:, :DI], 1)
    x = jnp.where(lax.axis_index("seq") == 0, x[0], x[1])
    taps = jnp.concatenate([x, conv[:, DI:]], axis=1)
    return jnp.pad(taps, ((0, 8 - taps.shape[0]), (0, 0)))


def all_taps(d_taps):
    d_taps = d_taps[: CK + 1]
    x, shared = d_taps[:, :IP], d_taps[:, IP:]
    first = lax.axis_index("seq") == 0
    none = jnp.zeros_like(x)
    even, odd = jnp.where(first, x, none), jnp.where(first, none, x)
    return jnp.concatenate([interleave(even, odd, 1), shared], axis=1).T


def all_heads(d_heads):
    first = lax.axis_index("seq") == 0
    none = jnp.zeros_like(d_heads)
    return interleave(jnp.where(first, d_heads, none), jnp.where(first, none, d_heads), 1)


def sum_heads(d_heads):
    count = lax.axis_size("dp")
    if count & (count - 1):
        return lax.psum(all_heads(d_heads), ("dp", "seq"))
    step = 1
    while step < count:
        d_heads = d_heads + lax.ppermute(d_heads, "dp", [(i, i ^ step) for i in range(count)])
        step *= 2
    other = sibling(d_heads)
    first = lax.axis_index("seq") == 0
    return interleave(jnp.where(first, d_heads, other), jnp.where(first, other, d_heads), 1)


def return_in(d_a, d_z, d_norm, d_gate, d_taps, rows):
    place = lax.axis_index("seq")
    first = place == 0
    values, width = small_width(rows)
    chips = d_a.shape[0] // (2 * rows)
    conv = all_taps(d_taps).reshape(2 * chips, values)
    conv = jnp.pad(conv, ((0, 0), (0, rows * width - values))).reshape(-1, width)
    small = jnp.concatenate([d_norm[:, None], d_gate[:, None], conv], axis=1)
    d_a = d_a + jnp.pad(small, ((0, 0), (SMALL, WA - SMALL - small.shape[1])))
    z_chip = scatter(d_z.astype(LOW))
    a_chip = scatter(d_a.astype(LOW))
    gate = a_chip[:, SMALL + 1].astype(F32)
    both = jnp.concatenate([a_chip, z_chip], axis=1)
    low, high = both[:rows], both[rows:]
    keep = jnp.where(first, low, high)
    other = sibling(jnp.where(first, high, low))
    total = keep.astype(F32) + other.astype(F32)
    even, odd = jnp.where(first, keep, other), jnp.where(first, other, keep)
    shard_in = jnp.concatenate(
        [
            interleave(even[:, WA:], odd[:, WA:], 1).astype(F32),
            interleave(even[:, :IP], odd[:, :IP], 1).astype(F32),
            total[:, IP:CP],
            interleave(even[:, CP:SMALL], odd[:, CP:SMALL], 1).astype(F32),
        ],
        axis=1,
    )
    small = total[:, SMALL:WA]
    norm = small[:, 0]
    conv = small[:, 2 : 2 + width].reshape(-1)[:values].reshape(-1, CK + 1)
    return shard_in, norm, conv, gate


def fetch_any(norm_low, in_low, conv_low, gate_low, out_low):
    norm, w_in, conv, gate, w_out = (
        lax.all_gather(v, ("dp", "seq"), axis=0, tiled=True)
        for v in (norm_low, in_low, conv_low, gate_low, out_low)
    )
    first = lax.axis_index("seq") == 0

    def mine(v, axis):
        parts = planes_of(v, axis)
        return jnp.where(first, parts[0], parts[1])

    w_a = jnp.concatenate(
        [
            mine(w_in[:, DI : 2 * DI], 1),
            w_in[:, 2 * DI : DI + CONV],
            mine(w_in[:, DI + CONV :], 1),
            jnp.zeros((w_in.shape[0], WA - SMALL), LOW),
        ],
        axis=1,
    )
    w_z = mine(w_in[:, :DI], 1)
    return (
        w_a,
        w_z,
        mine(w_out, 0),
        norm.astype(F32),
        mine(gate, 0).astype(F32),
        plane_taps(conv.astype(F32).T),
    )


def embed(v, axis):
    first = lax.axis_index("seq") == 0
    none = jnp.zeros_like(v)
    return interleave(jnp.where(first, v, none), jnp.where(first, none, v), axis)


def return_any(d_a, d_z, d_norm, d_gate, d_taps, d_out):
    def total(v):
        return lax.psum_scatter(v, ("dp", "seq"), scatter_dimension=0, tiled=True)

    d_in = jnp.concatenate(
        [embed(d_z, 1), embed(d_a[:, :IP], 1), d_a[:, IP:CP], embed(d_a[:, CP:SMALL], 1)], axis=1
    )
    return (
        total(d_in.astype(LOW)).astype(F32),
        total(d_norm),
        total(all_taps(d_taps)),
        total(embed(d_gate, 0)),
        total(embed(d_out, 0).astype(LOW)).astype(F32),
    )


def on_device(
    resid,
    segment_ids,
    cotangent,
    norm_gain,
    in_weight,
    conv_weight,
    gate_gain,
    out_weight,
    head_params,
    first_norm,
    first_in,
    first_conv,
    first_gate,
    first_out,
    first_head,
    second_norm,
    second_in,
    second_conv,
    second_gate,
    second_out,
    second_head,
):
    place = lax.axis_index("seq")
    local_rows = resid[0]
    cot_rows = cotangent[0]
    segments = segment_ids[0]
    tokens = segments.shape[0]
    one_head = out_weight.shape[0] == P_SIZE
    lows = [v.astype(LOW) for v in (norm_gain, in_weight, conv_weight, gate_gain, out_weight)]
    w_a, w_z, w_out, norm, gate, taps = (fetch if one_head else fetch_any)(*lows)

    all_rows = both_halves(local_rows)
    cot_half = both_halves(cot_rows.astype(LOW))
    heads = planes_of(head_params, 1)
    heads = jnp.pad(jnp.where(place == 0, heads[0], heads[1]), ((0, 5), (0, 0)))
    seg_col, seg_row = segments[:, None], segments[None, :]
    masks = [jnp.ones((tokens,), F32)]
    for back in range(1, CK):
        same = (segments[back:] == segments[:-back]).astype(F32)
        masks.append(jnp.concatenate([jnp.zeros((back,), F32), same]))
    mask = jnp.stack(masks, axis=1)

    def inverse_rms(values):
        return lax.rsqrt(jnp.mean(values * values, axis=-1, keepdims=True) + NORM_EPS)

    normed_half = (all_rows * inverse_rms(all_rows) * norm).astype(LOW)
    proj = mm(normed_half, w_a)
    pre, y = call(
        forward_kernel,
        [((tokens, CP), F32), ((tokens, IP), F32)],
        proj,
        taps,
        heads,
        seg_col,
        seg_row,
        mask,
    )
    z = mm(normed_half, w_z)
    grad_mixed = mm(cot_half, w_out, COLS_COLS)
    gated = y * (z * sigmoid(z))
    partial = jnp.stack(
        [jnp.sum(gated * gated, axis=1), jnp.sum(grad_mixed * gate * gated, axis=1)], axis=0
    )
    both = partial + sibling(partial)
    scale = lax.rsqrt(both[0] / DI + NORM_EPS)
    pull = scale * scale * scale * both[1] / DI
    mixed_half = (gated * scale[:, None] * gate).astype(LOW)
    d_out = mm(mixed_half, cot_half, ROWS_COLS)
    if one_head:
        d_out_low = d_out.astype(LOW)
        shard_out = scatter(d_out_low).astype(F32)
    result = local_rows + own_half(mm(mixed_half, w_out))
    sums = jnp.stack([scale, pull], axis=1)
    d_proj, d_z, d_taps, d_gate, d_heads = call(
        backward_kernel,
        [((tokens, WA), LOW), ((tokens, IP), LOW), ((8, CP), F32), ((1, IP), F32), ((3, HP), F32)],
        proj,
        z,
        pre,
        y,
        grad_mixed,
        sums,
        gate[None, :],
        taps,
        heads,
        seg_col,
        seg_row,
        mask,
    )
    head_total = sum_heads(d_heads)
    grad_normed = own_half(mm(d_proj, w_a, COLS_COLS) + mm(d_z, w_z, COLS_COLS))
    inv = inverse_rms(local_rows)
    weighted = grad_normed * norm
    dots = jnp.mean(weighted * local_rows, axis=-1, keepdims=True)
    grad_input = cot_rows + inv * weighted - local_rows * (inv * inv * inv * dots)
    d_norm = jnp.sum(grad_normed * local_rows * inv, axis=0)
    d_in_a = mm(normed_half, d_proj, ROWS_COLS)
    d_in_z = mm(normed_half, d_z, ROWS_COLS)
    if one_head:
        shard_in, shard_norm, shard_conv, shard_gate = return_in(
            d_in_a, d_in_z, d_norm, d_gate[0], d_taps, in_weight.shape[0]
        )
    else:
        shard_in, shard_norm, shard_conv, shard_gate, shard_out = return_any(
            d_in_a, d_in_z, d_norm, d_gate[0], d_taps, d_out
        )

    new_norm, new_first_norm, new_second_norm = adamw(
        norm_gain, shard_norm, first_norm, second_norm
    )
    new_in, new_first_in, new_second_in = adamw(in_weight, shard_in, first_in, second_in)
    new_conv, new_first_conv, new_second_conv = adamw(
        conv_weight, shard_conv, first_conv, second_conv
    )
    new_gate, new_first_gate, new_second_gate = adamw(
        gate_gain, shard_gate, first_gate, second_gate
    )
    new_out, new_first_out, new_second_out = adamw(out_weight, shard_out, first_out, second_out)
    new_head, new_first_head, new_second_head = adamw(
        head_params, head_total, first_head, second_head
    )
    return (
        result[None],
        grad_input[None],
        shard_norm,
        shard_in,
        shard_conv,
        shard_gate,
        shard_out,
        head_total,
        new_norm,
        new_in,
        new_conv,
        new_gate,
        new_out,
        new_head,
        new_first_norm,
        new_first_in,
        new_first_conv,
        new_first_gate,
        new_first_out,
        new_first_head,
        new_second_norm,
        new_second_in,
        new_second_conv,
        new_second_gate,
        new_second_out,
        new_second_head,
    )


def solution(mesh):
    rows = P(("dp", "seq"))
    wide = P(("dp", "seq"), None)
    tokens = P("dp", "seq", None)
    weights = (rows, wide, wide, rows, wide, P())
    return jax.shard_map(
        on_device,
        mesh=mesh,
        in_specs=(tokens, P("dp", None), tokens) + weights * 3,
        out_specs=(tokens, tokens) + weights_out() * 4,
        check_vma=False,
    )


def weights_out():
    rows = P(("dp", "seq"))
    wide = P(("dp", "seq"), None)
    return (rows, wide, wide, rows, wide, P())
```

```python
import functools

import jax
import jax.numpy as jnp
from jax import lax
from jax.experimental import pallas as pl
from jax.experimental.pallas import tpu as pltpu
from jax.sharding import PartitionSpec as P

H = 32
P_SIZE = 64
N = 128
CK = 4
BLOCK = 128
STEP = 4
DI = 2048
CONV = 2304


NORM_EPS = 1e-05
LEARNING_RATE = 0.02
BETA_FIRST = 0.9
BETA_SECOND = 0.95
ADAM_EPS = 1e-08
WEIGHT_DECAY = 0.1
HIGHEST = lax.Precision.HIGHEST
MASKED = -1e30
INTERPRET = False

PLANES = 2
HP = H // PLANES
IP = HP * P_SIZE
CP = IP + 2 * N
PAIR = 2 * P_SIZE
SMALL = CP + HP
WA = -(-(SMALL + 24) // 128) * 128
LOW = jnp.bfloat16
F32 = jnp.float32
ROWS_COLS = (((0,), (0,)), ((), ()))
COLS_COLS = (((1,), (1,)), ((), ()))


def mm(a, b, dims=(((1,), (0,)), ((), ()))):
    return lax.dot_general(a.astype(LOW), b.astype(LOW), dims, preferred_element_type=F32)


def exact_mm(a, b, dims=(((1,), (0,)), ((), ()))):
    return lax.dot_general(a, b, dims, precision=HIGHEST, preferred_element_type=F32)


def sibling(x):
    return lax.ppermute(x, "seq", [(0, 1), (1, 0)])


def both_halves(x):
    other = sibling(x)
    first = lax.axis_index("seq") == 0
    return jnp.concatenate([jnp.where(first, x, other), jnp.where(first, other, x)], axis=0)


def own_half(x):
    half = x.shape[0] // 2
    first = lax.axis_index("seq") == 0
    low, high = x[:half], x[half:]
    return jnp.where(first, low, high) + sibling(jnp.where(first, high, low))


def planes_of(x, axis):
    shape = x.shape
    width = shape[axis] // H
    split = x.reshape(shape[:axis] + (HP, PLANES, width) + shape[axis + 1 :])
    return [
        lax.index_in_dim(split, p, axis + 1, keepdims=False).reshape(
            shape[:axis] + (HP * width,) + shape[axis + 1 :]
        )
        for p in range(PLANES)
    ]


def interleave(even, odd, axis):
    shape = even.shape
    width = shape[axis] // HP
    parts = [
        v.reshape(shape[:axis] + (HP, 1, width) + shape[axis + 1 :]) for v in (even, odd)
    ]
    return jnp.concatenate(parts, axis=axis + 1).reshape(
        shape[:axis] + (H * width,) + shape[axis + 1 :]
    )


def adamw(weight, gradient, first_moment, second_moment):
    first_new = BETA_FIRST * first_moment + (1.0 - BETA_FIRST) * gradient
    second_new = BETA_SECOND * second_moment + (1.0 - BETA_SECOND) * gradient * gradient
    first_hat = first_new / (1.0 - BETA_FIRST**STEP)
    second_hat = second_new / (1.0 - BETA_SECOND**STEP)
    weight_new = weight - LEARNING_RATE * (
        first_hat / (jnp.sqrt(second_hat) + ADAM_EPS) + WEIGHT_DECAY * weight
    )
    return (weight_new, first_new, second_new)


def sigmoid(v):
    return 1.0 / (1.0 + jnp.exp(-v))


def softplus(v):
    return jnp.maximum(v, 0.0) + jnp.log1p(jnp.exp(-jnp.abs(v)))


def lower_ones(length):
    row = lax.broadcasted_iota(jnp.int32, (length, length), 0)
    col = lax.broadcasted_iota(jnp.int32, (length, length), 1)
    return (row >= col).astype(F32)


def column(values, index):
    return values[:, index : index + 1]


def per_pair(values, pair, lanes_low):
    return jnp.where(lanes_low, column(values, 2 * pair), column(values, 2 * pair + 1))


def steps_of(dt_raw, heads):
    raw = dt_raw + heads[1:2, :]
    timestep = softplus(raw)
    decay = -jnp.exp(heads[0:1, :]) * timestep
    return raw, timestep, decay


def block_sums(decay):
    ones = lower_ones(BLOCK)
    columns, rows = [], []
    for b in range(decay.shape[0] // BLOCK):
        part = decay[b * BLOCK : (b + 1) * BLOCK]
        columns.append(exact_mm(ones, part))
        rows.append(exact_mm(part, ones, (((0,), (1,)), ((), ()))))
    return columns, rows


def visible_in(seg_col, seg_row, b):
    span = slice(b * BLOCK, (b + 1) * BLOCK)
    row = lax.broadcasted_iota(jnp.int32, (BLOCK, BLOCK), 0)
    col = lax.broadcasted_iota(jnp.int32, (BLOCK, BLOCK), 1)
    return (seg_col[span] == seg_row[:, span]) & (row >= col)


def across(seg_col, seg_row, b):
    return seg_col[b * BLOCK : (b + 1) * BLOCK] == seg_row[:, (b - 1) * BLOCK : b * BLOCK]


def forward_kernel(proj_ref, taps_ref, heads_ref, segc_ref, segr_ref, mask_ref, pre_ref, y_ref):
    tokens = proj_ref.shape[0]
    blocks = tokens // BLOCK
    heads = heads_ref[...]
    seg_col, seg_row = segc_ref[...], segr_ref[...]
    mask = mask_ref[...]
    taps = taps_ref[...]

    def convolve(lanes):
        source = proj_ref[:, lanes]
        total = taps[CK : CK + 1, lanes] + taps[CK - 1 : CK, lanes] * source
        for back in range(1, CK):
            moved = pltpu.roll(source, back, 0) * column(mask, back)
            total = total + taps[CK - 1 - back : CK - back, lanes] * moved
        pre_ref[:, lanes] = total
        return total * sigmoid(total)

    write_rows = convolve(slice(IP, IP + N))
    read_rows = convolve(slice(IP + N, CP))
    _, timestep, decay = steps_of(proj_ref[:, CP : CP + HP], heads)
    sums_col, sums_row = block_sums(decay)
    affinity, crossing = [], [None]
    for b in range(blocks):
        span = slice(b * BLOCK, (b + 1) * BLOCK)
        affinity.append(mm(read_rows[span], write_rows[span], COLS_COLS))
        if b:
            before = slice((b - 1) * BLOCK, b * BLOCK)
            crossing.append(
                jnp.where(
                    across(seg_col, seg_row, b), mm(read_rows[span], write_rows[before], COLS_COLS), 0.0
                ).astype(LOW)
            )
    seen = [visible_in(seg_col, seg_row, b) for b in range(blocks)]
    lanes_low = lax.broadcasted_iota(jnp.int32, (1, PAIR), 1) < P_SIZE
    entry = [jnp.exp(c) for c in sums_col]
    tail = [jnp.exp(c[BLOCK - 1 : BLOCK, :] - c) for c in sums_col]
    for pair in range(HP // 2):
        lanes = slice(pair * PAIR, (pair + 1) * PAIR)
        inputs = convolve(lanes)
        scaled = inputs * per_pair(timestep, pair, lanes_low)
        skip = jnp.where(lanes_low, heads[2:3, 2 * pair : 2 * pair + 1], heads[2:3, 2 * pair + 1 : 2 * pair + 2])
        for b in range(blocks):
            span = slice(b * BLOCK, (b + 1) * BLOCK)
            scores = []
            for h in (2 * pair, 2 * pair + 1):
                spread = column(sums_col[b], h) - sums_row[b][h : h + 1, :]
                scores.append((affinity[b] * jnp.exp(jnp.where(seen[b], spread, MASKED))).astype(LOW))
            here = scaled[span]
            stacked = jnp.concatenate(
                [jnp.where(lanes_low, here, 0.0), jnp.where(lanes_low, 0.0, here)], axis=0
            )
            out = mm(jnp.concatenate(scores, axis=1), stacked)
            if b:
                before = slice((b - 1) * BLOCK, b * BLOCK)
                weighted = scaled[before] * per_pair(tail[b - 1], pair, lanes_low)
                out = out + per_pair(entry[b], pair, lanes_low) * mm(crossing[b], weighted)
            y_ref[span, lanes] = out + skip * inputs[span]


def backward_kernel(
    proj_ref,
    z_ref,
    pre_ref,
    y_ref,
    gm_ref,
    sums_ref,
    gate_ref,
    taps_ref,
    heads_ref,
    segc_ref,
    segr_ref,
    mask_ref,
    da_ref,
    dz_ref,
    dtaps_ref,
    dgate_ref,
    dheads_ref,
):
    tokens = proj_ref.shape[0]
    blocks = tokens // BLOCK
    heads = heads_ref[...]
    seg_col, seg_row = segc_ref[...], segr_ref[...]
    mask = mask_ref[...]
    taps = taps_ref[...]
    scale = sums_ref[:, 0:1]
    pull = sums_ref[:, 1:2]

    def activate(lanes):
        pre = pre_ref[:, lanes]
        sig = sigmoid(pre)
        return pre * sig, sig * (1.0 + pre * (1.0 - sig))

    def unconvolve(lanes, grad):
        source = proj_ref[:, lanes]
        result = taps[CK - 1 : CK, lanes] * grad
        dtaps_ref[CK : CK + 1, lanes] = jnp.sum(grad, axis=0, keepdims=True)
        dtaps_ref[CK - 1 : CK, lanes] = jnp.sum(grad * source, axis=0, keepdims=True)
        for back in range(1, CK):
            at = CK - 1 - back
            kept = grad * column(mask, back)
            moved = pltpu.roll(kept, tokens - back, 0)
            dtaps_ref[at : at + 1, lanes] = jnp.sum(moved * source, axis=0, keepdims=True)
            result = result + taps[at : at + 1, lanes] * moved
        da_ref[:, lanes] = result.astype(LOW)

    write_rows, write_slope = activate(slice(IP, IP + N))
    read_rows, read_slope = activate(slice(IP + N, CP))
    raw, timestep, decay = steps_of(proj_ref[:, CP : CP + HP], heads)
    sums_col, sums_row = block_sums(decay)
    affinity, crossing = [], [None]
    for b in range(blocks):
        span = slice(b * BLOCK, (b + 1) * BLOCK)
        affinity.append(mm(read_rows[span], write_rows[span], COLS_COLS))
        if b:
            before = slice((b - 1) * BLOCK, b * BLOCK)
            crossing.append(
                jnp.where(
                    across(seg_col, seg_row, b), mm(read_rows[span], write_rows[before], COLS_COLS), 0.0
                ).astype(LOW)
            )
    seen = [visible_in(seg_col, seg_row, b) for b in range(blocks)]
    lanes_low = lax.broadcasted_iota(jnp.int32, (1, PAIR), 1) < P_SIZE
    head_lane = lax.broadcasted_iota(jnp.int32, (1, HP), 1)
    entry = [jnp.exp(c) for c in sums_col]
    tail = [jnp.exp(c[BLOCK - 1 : BLOCK, :] - c) for c in sums_col]
    d_affinity = [jnp.zeros((BLOCK, BLOCK), F32) for _ in range(blocks)]
    d_crossing = [jnp.zeros((BLOCK, BLOCK), F32) for _ in range(blocks)]
    d_sums = [jnp.zeros((BLOCK, HP), F32) for _ in range(blocks)]
    d_steps = [jnp.zeros((BLOCK, HP), F32) for _ in range(blocks)]
    d_skip = jnp.zeros((1, HP), F32)

    def spread_heads(values, pair):
        low = jnp.sum(jnp.where(lanes_low, values, 0.0), axis=1, keepdims=True)
        high = jnp.sum(jnp.where(lanes_low, 0.0, values), axis=1, keepdims=True)
        return jnp.where(head_lane == 2 * pair, low, 0.0) + jnp.where(
            head_lane == 2 * pair + 1, high, 0.0
        )

    for pair in range(HP // 2):
        lanes = slice(pair * PAIR, (pair + 1) * PAIR)
        inputs, slope = activate(lanes)
        step = per_pair(timestep, pair, lanes_low)
        scaled = inputs * step
        skip = jnp.where(lanes_low, heads[2:3, 2 * pair : 2 * pair + 1], heads[2:3, 2 * pair + 1 : 2 * pair + 2])
        z = z_ref[:, lanes]
        sig = sigmoid(z)
        silu = z * sig
        y = y_ref[:, lanes]
        gated = y * silu
        gm = gm_ref[:, lanes]
        dgate_ref[:, lanes] = jnp.sum(gm * gated * scale, axis=0, keepdims=True)
        d_gated = scale * (gm * gate_ref[:, lanes]) - gated * pull
        dz_ref[:, lanes] = (d_gated * y * (sig * (1.0 + z * (1.0 - sig)))).astype(LOW)
        d_y = d_gated * silu
        d_skip = d_skip + jnp.sum(spread_heads(d_y * inputs, pair), axis=0, keepdims=True)
        d_y_low = d_y.astype(LOW)
        d_y_round = d_y_low.astype(F32)
        scan = y - skip * inputs
        scaled_low = scaled.astype(LOW)
        scaled_round = scaled_low.astype(F32)
        d_scaled = [None] * blocks
        for b in range(blocks):
            span = slice(b * BLOCK, (b + 1) * BLOCK)
            grads, here = d_y_round[span], scaled_low[span]
            stacked = jnp.concatenate(
                [jnp.where(lanes_low, grads, 0.0), jnp.where(lanes_low, 0.0, grads)], axis=0
            ).astype(LOW)
            d_scores = mm(stacked, here, COLS_COLS)
            scores = []
            for i, h in enumerate((2 * pair, 2 * pair + 1)):
                spread = column(sums_col[b], h) - sums_row[b][h : h + 1, :]
                fade = jnp.exp(jnp.where(seen[b], spread, MASKED))
                d_affinity[b] = d_affinity[b] + d_scores[i * BLOCK : (i + 1) * BLOCK] * fade
                scores.append((affinity[b] * fade).astype(LOW))
            d_here = mm(jnp.concatenate(scores, axis=0), stacked, ROWS_COLS)
            d_scaled[b] = d_here if d_scaled[b] is None else d_scaled[b] + d_here
            d_sums[b] = d_sums[b] + spread_heads(grads * scan[span], pair)
            if b:
                before = slice((b - 1) * BLOCK, b * BLOCK)
                tail_here = per_pair(tail[b - 1], pair, lanes_low)
                weighted = (scaled[before] * tail_here).astype(LOW)
                incoming = (d_y[span] * per_pair(entry[b], pair, lanes_low)).astype(LOW)
                d_weighted = mm(crossing[b], incoming, ROWS_COLS)
                d_crossing[b] = d_crossing[b] + mm(incoming, weighted, COLS_COLS)
                d_scaled[b - 1] = d_scaled[b - 1] + tail_here * d_weighted
        for b in range(blocks):
            span = slice(b * BLOCK, (b + 1) * BLOCK)
            d_sums[b] = d_sums[b] - spread_heads(scaled_round[span] * d_scaled[b], pair)
            d_steps[b] = d_steps[b] + spread_heads(inputs[span] * d_scaled[b], pair)
        d_inputs = jnp.concatenate(d_scaled, axis=0) * step + skip * d_y
        unconvolve(lanes, d_inputs * slope)

    ones = lower_ones(BLOCK)
    d_write = [jnp.zeros((BLOCK, N), F32) for _ in range(blocks)]
    d_read = [None] * blocks
    d_decay = [None] * blocks
    later = jnp.zeros((1, HP), F32)
    for b in range(blocks):
        span = slice(b * BLOCK, (b + 1) * BLOCK)
        d_read[b] = mm(d_affinity[b], write_rows[span])
        d_write[b] = d_write[b] + mm(d_affinity[b], read_rows[span], ROWS_COLS)
        if b:
            before = slice((b - 1) * BLOCK, b * BLOCK)
            kept = jnp.where(across(seg_col, seg_row, b), d_crossing[b], 0.0)
            d_read[b] = d_read[b] + mm(kept, write_rows[before])
            d_write[b - 1] = d_write[b - 1] + mm(kept, read_rows[span], ROWS_COLS)
    for b in reversed(range(blocks)):
        d_decay[b] = exact_mm(ones, d_sums[b], ROWS_COLS) + later
        later = later + jnp.sum(d_sums[b], axis=0, keepdims=True)
    unconvolve(slice(IP, IP + N), jnp.concatenate(d_write, axis=0) * write_slope)
    unconvolve(slice(IP + N, CP), jnp.concatenate(d_read, axis=0) * read_slope)
    d_decay = jnp.concatenate(d_decay, axis=0)
    d_raw = (jnp.concatenate(d_steps, axis=0) - d_decay * jnp.exp(heads[0:1, :])) * sigmoid(raw)
    padding = jnp.zeros((tokens, WA - SMALL), LOW)
    da_ref[:, CP:WA] = jnp.concatenate([d_raw.astype(LOW), padding], axis=1)
    dheads_ref[0:1, :] = jnp.sum(d_decay * decay, axis=0, keepdims=True)
    dheads_ref[1:2, :] = jnp.sum(d_raw, axis=0, keepdims=True)
    dheads_ref[2:3, :] = d_skip


def call(kernel, outs, *args):
    return pl.pallas_call(
        kernel,
        out_shape=[jax.ShapeDtypeStruct(shape, kind) for shape, kind in outs],
        interpret=INTERPRET,
    )(*args)


def swap(x, by):
    return lax.ppermute(x, "dp", [(i, i ^ by) for i in range(lax.axis_size("dp"))])


def place_kernel(bounds, at_ref, *refs):
    sources, outs = refs[: 1 - len(bounds)], refs[1 - len(bounds) :]
    chip = at_ref[0]
    rows = outs[0].shape[0] // 16
    block = 0
    for source in sources:
        for i in range(source.shape[0] // rows):
            k, j = block // 4, block % 4
            to = pl.multiple_of((chip ^ (4 * j + k)) * rows, rows)
            for out_ref, low, high in zip(outs, bounds[:-1], bounds[1:]):
                out_ref[pl.ds(to, rows), :] = source[i * rows : (i + 1) * rows, low:high]
            block += 1


def put(cuts, *sources):
    rows = sum(v.shape[0] for v in sources)
    bounds = (0,) + cuts + (sources[0].shape[1],)
    return pl.pallas_call(
        functools.partial(place_kernel, bounds),
        out_shape=[
            jax.ShapeDtypeStruct((rows, high - low), sources[0].dtype)
            for low, high in zip(bounds[:-1], bounds[1:])
        ],
        in_specs=[pl.BlockSpec(memory_space=pltpu.SMEM)] + [pl.BlockSpec()] * len(sources),
        interpret=INTERPRET,
    )(lax.axis_index("dp")[None].astype(jnp.int32), *sources)


def gather(x, *cuts):
    mine = jnp.concatenate([x] + [swap(x, 4 * j) for j in range(1, 4)], axis=0)
    half = mine.shape[0] // 2
    by_x, by_y = swap(mine, 1), swap(mine, 2)
    return put(cuts, mine, by_x, by_y, swap(by_y[:half], 1), swap(by_x[half:], 2))


def scatter(x):
    chip = lax.axis_index("dp")
    plane, depth = chip % 4, chip // 4
    rows = x.shape[0] // 16
    blocks = x.reshape(4, 4, rows, x.shape[1])

    def block(k):
        return lax.dynamic_index_in_dim(blocks, plane ^ k, 1, keepdims=False)

    far = block(3)
    from_x, from_y = swap(far[:2], 1), swap(far[2:], 2)

    def add(first, *others):
        total = first.astype(F32)
        for v in others:
            total = total + v.astype(F32)
        return total

    near_x, near_y = block(1), block(2)
    to_x = jnp.concatenate([near_x[:2], add(near_x[2:], from_y).astype(LOW)], axis=0)
    to_y = jnp.concatenate([add(near_y[:2], from_x).astype(LOW), near_y[2:]], axis=0)
    column_sum = add(block(0), swap(to_x, 1), swap(to_y, 2))

    def layer(j):
        return lax.dynamic_index_in_dim(column_sum, depth ^ j, 0, keepdims=False)

    return add(layer(0), *[swap(layer(j).astype(LOW), 4 * j) for j in range(1, 4)])


def small_width(rows):
    per_core = CONV // (DI // P_SIZE)
    return per_core * (CK + 1), -(-(per_core * (CK + 1)) // rows)


def fetch(norm_low, in_low, conv_low, gate_low, out_low):
    place = lax.axis_index("seq")
    rows = in_low.shape[0]
    values, width = small_width(rows)
    z = planes_of(in_low[:, :DI], 1)
    x = planes_of(in_low[:, DI : 2 * DI], 1)
    shared = in_low[:, 2 * DI : DI + CONV]
    steps = planes_of(in_low[:, DI + CONV :], 1)
    conv_flat = jnp.pad(conv_low.reshape(-1), (0, rows * width - values)).reshape(rows, width)
    gate_two = gate_low.reshape(2, rows).T
    payload = []
    for p in range(PLANES):
        gate_here = jnp.where(place == p, gate_two, jnp.zeros_like(gate_two))
        pieces = [x[p], shared, steps[p], norm_low[:, None], gate_here, conv_flat]
        used = SMALL + 3 + width
        pieces.append(jnp.zeros((rows, WA - used), LOW))
        pieces.append(z[p])
        payload.append(jnp.concatenate(pieces, axis=1))
    first = place == 0
    mine = jnp.where(first, payload[0], payload[1])
    other = sibling(jnp.where(first, payload[1], payload[0]))
    chip = jnp.concatenate([jnp.where(first, mine, other), jnp.where(first, other, mine)], axis=0)
    (w_a,) = gather(chip[:, :WA])
    w_z, w_out = gather(jnp.concatenate([chip[:, WA:], out_low], axis=1), IP)
    chips = w_a.shape[0] // (2 * rows)
    small = w_a[:, SMALL : SMALL + 3 + width].astype(F32)
    norm = small[:, 0]
    gate = small[:, 1:3].reshape(chips, 2, rows, 2).sum(1).transpose(0, 2, 1).reshape(-1)
    conv = small[:, 3:].reshape(2 * chips, rows * width)[:, :values].reshape(CONV, CK + 1).T
    return w_a, w_z, w_out, norm, gate, plane_taps(conv)


def plane_taps(conv):
    x = planes_of(conv[:, :DI], 1)
    x = jnp.where(lax.axis_index("seq") == 0, x[0], x[1])
    taps = jnp.concatenate([x, conv[:, DI:]], axis=1)
    return jnp.pad(taps, ((0, 8 - taps.shape[0]), (0, 0)))


def all_taps(d_taps):
    d_taps = d_taps[: CK + 1]
    x, shared = d_taps[:, :IP], d_taps[:, IP:]
    first = lax.axis_index("seq") == 0
    none = jnp.zeros_like(x)
    even, odd = jnp.where(first, x, none), jnp.where(first, none, x)
    return jnp.concatenate([interleave(even, odd, 1), shared], axis=1).T


def all_heads(d_heads):
    first = lax.axis_index("seq") == 0
    none = jnp.zeros_like(d_heads)
    return interleave(jnp.where(first, d_heads, none), jnp.where(first, none, d_heads), 1)


def sum_heads(d_heads):
    count = lax.axis_size("dp")
    if count & (count - 1):
        return lax.psum(all_heads(d_heads), ("dp", "seq"))
    step = 1
    while step < count:
        d_heads = d_heads + lax.ppermute(d_heads, "dp", [(i, i ^ step) for i in range(count)])
        step *= 2
    other = sibling(d_heads)
    first = lax.axis_index("seq") == 0
    return interleave(jnp.where(first, d_heads, other), jnp.where(first, other, d_heads), 1)


def return_in(d_a, d_z, d_norm, d_gate, d_taps, rows):
    place = lax.axis_index("seq")
    first = place == 0
    values, width = small_width(rows)
    chips = d_a.shape[0] // (2 * rows)
    conv = all_taps(d_taps).reshape(2 * chips, values)
    conv = jnp.pad(conv, ((0, 0), (0, rows * width - values))).reshape(-1, width)
    small = jnp.concatenate([d_norm[:, None], d_gate[:, None], conv], axis=1)
    d_a = d_a + jnp.pad(small, ((0, 0), (SMALL, WA - SMALL - small.shape[1])))
    z_chip = scatter(d_z.astype(LOW))
    a_chip = scatter(d_a.astype(LOW))
    gate = a_chip[:, SMALL + 1].astype(F32)
    both = jnp.concatenate([a_chip, z_chip], axis=1)
    low, high = both[:rows], both[rows:]
    keep = jnp.where(first, low, high)
    other = sibling(jnp.where(first, high, low))
    total = keep.astype(F32) + other.astype(F32)
    even, odd = jnp.where(first, keep, other), jnp.where(first, other, keep)
    shard_in = jnp.concatenate(
        [
            interleave(even[:, WA:], odd[:, WA:], 1).astype(F32),
            interleave(even[:, :IP], odd[:, :IP], 1).astype(F32),
            total[:, IP:CP],
            interleave(even[:, CP:SMALL], odd[:, CP:SMALL], 1).astype(F32),
        ],
        axis=1,
    )
    small = total[:, SMALL:WA]
    norm = small[:, 0]
    conv = small[:, 2 : 2 + width].reshape(-1)[:values].reshape(-1, CK + 1)
    return shard_in, norm, conv, gate


def fetch_any(norm_low, in_low, conv_low, gate_low, out_low):
    norm, w_in, conv, gate, w_out = (
        lax.all_gather(v, ("dp", "seq"), axis=0, tiled=True)
        for v in (norm_low, in_low, conv_low, gate_low, out_low)
    )
    first = lax.axis_index("seq") == 0

    def mine(v, axis):
        parts = planes_of(v, axis)
        return jnp.where(first, parts[0], parts[1])

    w_a = jnp.concatenate(
        [
            mine(w_in[:, DI : 2 * DI], 1),
            w_in[:, 2 * DI : DI + CONV],
            mine(w_in[:, DI + CONV :], 1),
            jnp.zeros((w_in.shape[0], WA - SMALL), LOW),
        ],
        axis=1,
    )
    w_z = mine(w_in[:, :DI], 1)
    return (
        w_a,
        w_z,
        mine(w_out, 0),
        norm.astype(F32),
        mine(gate, 0).astype(F32),
        plane_taps(conv.astype(F32).T),
    )


def embed(v, axis):
    first = lax.axis_index("seq") == 0
    none = jnp.zeros_like(v)
    return interleave(jnp.where(first, v, none), jnp.where(first, none, v), axis)


def return_any(d_a, d_z, d_norm, d_gate, d_taps, d_out):
    def total(v):
        return lax.psum_scatter(v, ("dp", "seq"), scatter_dimension=0, tiled=True)

    d_in = jnp.concatenate(
        [embed(d_z, 1), embed(d_a[:, :IP], 1), d_a[:, IP:CP], embed(d_a[:, CP:SMALL], 1)], axis=1
    )
    return (
        total(d_in.astype(LOW)).astype(F32),
        total(d_norm),
        total(all_taps(d_taps)),
        total(embed(d_gate, 0)),
        total(embed(d_out, 0).astype(LOW)).astype(F32),
    )


def on_device(
    resid,
    segment_ids,
    cotangent,
    norm_gain,
    in_weight,
    conv_weight,
    gate_gain,
    out_weight,
    head_params,
    first_norm,
    first_in,
    first_conv,
    first_gate,
    first_out,
    first_head,
    second_norm,
    second_in,
    second_conv,
    second_gate,
    second_out,
    second_head,
):
    place = lax.axis_index("seq")
    local_rows = resid[0]
    cot_rows = cotangent[0]
    segments = segment_ids[0]
    tokens = segments.shape[0]
    one_head = out_weight.shape[0] == P_SIZE and lax.axis_size("dp") == 16
    lows = [v.astype(LOW) for v in (norm_gain, in_weight, conv_weight, gate_gain, out_weight)]
    w_a, w_z, w_out, norm, gate, taps = (fetch if one_head else fetch_any)(*lows)

    all_rows = both_halves(local_rows)
    cot_half = both_halves(cot_rows.astype(LOW))
    heads = planes_of(head_params, 1)
    heads = jnp.pad(jnp.where(place == 0, heads[0], heads[1]), ((0, 5), (0, 0)))
    seg_col, seg_row = segments[:, None], segments[None, :]
    masks = [jnp.ones((tokens,), F32)]
    for back in range(1, CK):
        same = (segments[back:] == segments[:-back]).astype(F32)
        masks.append(jnp.concatenate([jnp.zeros((back,), F32), same]))
    mask = jnp.stack(masks, axis=1)

    def inverse_rms(values):
        return lax.rsqrt(jnp.mean(values * values, axis=-1, keepdims=True) + NORM_EPS)

    normed_half = (all_rows * inverse_rms(all_rows) * norm).astype(LOW)
    proj = mm(normed_half, w_a)
    pre, y = call(
        forward_kernel,
        [((tokens, CP), F32), ((tokens, IP), F32)],
        proj,
        taps,
        heads,
        seg_col,
        seg_row,
        mask,
    )
    z = mm(normed_half, w_z)
    grad_mixed = mm(cot_half, w_out, COLS_COLS)
    gated = y * (z * sigmoid(z))
    partial = jnp.stack(
        [jnp.sum(gated * gated, axis=1), jnp.sum(grad_mixed * gate * gated, axis=1)], axis=0
    )
    both = partial + sibling(partial)
    scale = lax.rsqrt(both[0] / DI + NORM_EPS)
    pull = scale * scale * scale * both[1] / DI
    mixed_half = (gated * scale[:, None] * gate).astype(LOW)
    d_out = mm(mixed_half, cot_half, ROWS_COLS)
    if one_head:
        d_out_low = d_out.astype(LOW)
        shard_out = scatter(d_out_low).astype(F32)
    result = local_rows + own_half(mm(mixed_half, w_out))
    sums = jnp.stack([scale, pull], axis=1)
    d_proj, d_z, d_taps, d_gate, d_heads = call(
        backward_kernel,
        [((tokens, WA), LOW), ((tokens, IP), LOW), ((8, CP), F32), ((1, IP), F32), ((3, HP), F32)],
        proj,
        z,
        pre,
        y,
        grad_mixed,
        sums,
        gate[None, :],
        taps,
        heads,
        seg_col,
        seg_row,
        mask,
    )
    head_total = sum_heads(d_heads)
    grad_normed = own_half(mm(d_proj, w_a, COLS_COLS) + mm(d_z, w_z, COLS_COLS))
    inv = inverse_rms(local_rows)
    weighted = grad_normed * norm
    dots = jnp.mean(weighted * local_rows, axis=-1, keepdims=True)
    grad_input = cot_rows + inv * weighted - local_rows * (inv * inv * inv * dots)
    d_norm = jnp.sum(grad_normed * local_rows * inv, axis=0)
    d_in_a = mm(normed_half, d_proj, ROWS_COLS)
    d_in_z = mm(normed_half, d_z, ROWS_COLS)
    if one_head:
        shard_in, shard_norm, shard_conv, shard_gate = return_in(
            d_in_a, d_in_z, d_norm, d_gate[0], d_taps, in_weight.shape[0]
        )
    else:
        shard_in, shard_norm, shard_conv, shard_gate, shard_out = return_any(
            d_in_a, d_in_z, d_norm, d_gate[0], d_taps, d_out
        )

    new_norm, new_first_norm, new_second_norm = adamw(
        norm_gain, shard_norm, first_norm, second_norm
    )
    new_in, new_first_in, new_second_in = adamw(in_weight, shard_in, first_in, second_in)
    new_conv, new_first_conv, new_second_conv = adamw(
        conv_weight, shard_conv, first_conv, second_conv
    )
    new_gate, new_first_gate, new_second_gate = adamw(
        gate_gain, shard_gate, first_gate, second_gate
    )
    new_out, new_first_out, new_second_out = adamw(out_weight, shard_out, first_out, second_out)
    new_head, new_first_head, new_second_head = adamw(
        head_params, head_total, first_head, second_head
    )
    return (
        result[None],
        grad_input[None],
        shard_norm,
        shard_in,
        shard_conv,
        shard_gate,
        shard_out,
        head_total,
        new_norm,
        new_in,
        new_conv,
        new_gate,
        new_out,
        new_head,
        new_first_norm,
        new_first_in,
        new_first_conv,
        new_first_gate,
        new_first_out,
        new_first_head,
        new_second_norm,
        new_second_in,
        new_second_conv,
        new_second_gate,
        new_second_out,
        new_second_head,
    )


def solution(mesh):
    rows = P(("dp", "seq"))
    wide = P(("dp", "seq"), None)
    tokens = P("dp", "seq", None)
    weights = (rows, wide, wide, rows, wide, P())
    return jax.shard_map(
        on_device,
        mesh=mesh,
        in_specs=(tokens, P("dp", None), tokens) + weights * 3,
        out_specs=(tokens, tokens) + weights_out() * 4,
        check_vma=False,
    )


def weights_out():
    rows = P(("dp", "seq"))
    wide = P(("dp", "seq"), None)
    return (rows, wide, wide, rows, wide, P())
```

```python
import functools

import jax
import jax.numpy as jnp
from jax import lax
from jax.experimental import pallas as pl
from jax.experimental.pallas import tpu as pltpu
from jax.sharding import PartitionSpec as P


H = 32
P_SIZE = 64
N = 128
CK = 4
BLOCK = 128
STEP = 4
DI = 2048
CONV = 2304


NORM_EPS = 1e-05
LEARNING_RATE = 0.02
BETA_FIRST = 0.9
BETA_SECOND = 0.95
ADAM_EPS = 1e-08
WEIGHT_DECAY = 0.1
HIGHEST = lax.Precision.HIGHEST
MASKED = -1e30
INTERPRET = False

PLANES = 2
HP = H // PLANES
IP = HP * P_SIZE
CP = IP + 2 * N
PAIR = 2 * P_SIZE
WT = 2 * N + 128
SMALL = 2 * N + HP
NOTE_WIDTH = 16
LOW = jnp.bfloat16
F32 = jnp.float32
NORMAL = (((1,), (0,)), ((), ()))
ROWS_COLS = (((0,), (0,)), ((), ()))
COLS_COLS = (((1,), (1,)), ((), ()))


def mm(a, b, dims=(((1,), (0,)), ((), ()))):
    return lax.dot_general(a.astype(LOW), b.astype(LOW), dims, preferred_element_type=F32)


def exact_mm(a, b, dims=(((1,), (0,)), ((), ()))):
    return lax.dot_general(a, b, dims, precision=HIGHEST, preferred_element_type=F32)


def sibling(x):
    return lax.ppermute(x, "seq", [(0, 1), (1, 0)])


def both_halves(x):
    other = sibling(x)
    first = lax.axis_index("seq") == 0
    return jnp.concatenate([jnp.where(first, x, other), jnp.where(first, other, x)], axis=0)


def own_half(x):
    half = x.shape[0] // 2
    first = lax.axis_index("seq") == 0
    low, high = x[:half], x[half:]
    return jnp.where(first, low, high) + sibling(jnp.where(first, high, low))


def planes_of(x, axis):
    shape = x.shape
    width = shape[axis] // H
    split = x.reshape(shape[:axis] + (HP, PLANES, width) + shape[axis + 1 :])
    return [
        lax.index_in_dim(split, p, axis + 1, keepdims=False).reshape(
            shape[:axis] + (HP * width,) + shape[axis + 1 :]
        )
        for p in range(PLANES)
    ]


def interleave(even, odd, axis):
    shape = even.shape
    width = shape[axis] // HP
    parts = [
        v.reshape(shape[:axis] + (HP, 1, width) + shape[axis + 1 :]) for v in (even, odd)
    ]
    return jnp.concatenate(parts, axis=axis + 1).reshape(
        shape[:axis] + (H * width,) + shape[axis + 1 :]
    )


def adamw(weight, gradient, first_moment, second_moment):
    first_new = BETA_FIRST * first_moment + (1.0 - BETA_FIRST) * gradient
    second_new = BETA_SECOND * second_moment + (1.0 - BETA_SECOND) * gradient * gradient
    first_hat = first_new / (1.0 - BETA_FIRST**STEP)
    second_hat = second_new / (1.0 - BETA_SECOND**STEP)
    weight_new = weight - LEARNING_RATE * (
        first_hat / (jnp.sqrt(second_hat) + ADAM_EPS) + WEIGHT_DECAY * weight
    )
    return (weight_new, first_new, second_new)


def sigmoid(v):
    return 1.0 / (1.0 + jnp.exp(-v))


def softplus(v):
    return jnp.maximum(v, 0.0) + jnp.log1p(jnp.exp(-jnp.abs(v)))


def lower_ones(length):
    row = lax.broadcasted_iota(jnp.int32, (length, length), 0)
    col = lax.broadcasted_iota(jnp.int32, (length, length), 1)
    return (row >= col).astype(F32)


def column(values, index):
    return values[:, index : index + 1]


def per_pair(values, pair, lanes_low):
    return jnp.where(lanes_low, column(values, 2 * pair), column(values, 2 * pair + 1))


def steps_of(dt_raw, heads):
    raw = dt_raw + heads[1:2, :]
    timestep = softplus(raw)
    decay = -jnp.exp(heads[0:1, :]) * timestep
    return raw, timestep, decay


def block_sums(decay):
    ones = lower_ones(BLOCK)
    columns, rows = [], []
    for b in range(decay.shape[0] // BLOCK):
        part = decay[b * BLOCK : (b + 1) * BLOCK]
        columns.append(exact_mm(ones, part))
        rows.append(exact_mm(part, ones, (((0,), (1,)), ((), ()))))
    return columns, rows


def visible_in(seg_col, seg_row, b):
    span = slice(b * BLOCK, (b + 1) * BLOCK)
    row = lax.broadcasted_iota(jnp.int32, (BLOCK, BLOCK), 0)
    col = lax.broadcasted_iota(jnp.int32, (BLOCK, BLOCK), 1)
    return (seg_col[span] == seg_row[:, span]) & (row >= col)


def across(seg_col, seg_row, b):
    return seg_col[b * BLOCK : (b + 1) * BLOCK] == seg_row[:, (b - 1) * BLOCK : b * BLOCK]


def source_of(px_ref, pt_ref, lanes):
    if lanes.start < IP:
        return px_ref[:, lanes]
    return pt_ref[:, lanes.start - IP : lanes.stop - IP]


def forward_kernel(px_ref, pt_ref, taps_ref, heads_ref, segc_ref, segr_ref, mask_ref, pre_ref, y_ref):
    tokens = px_ref.shape[0]
    blocks = tokens // BLOCK
    heads = heads_ref[...]
    seg_col, seg_row = segc_ref[...], segr_ref[...]
    mask = mask_ref[...]
    taps = taps_ref[...]

    def convolve(lanes):
        source = source_of(px_ref, pt_ref, lanes)
        total = taps[CK : CK + 1, lanes] + taps[CK - 1 : CK, lanes] * source
        for back in range(1, CK):
            moved = pltpu.roll(source, back, 0) * column(mask, back)
            total = total + taps[CK - 1 - back : CK - back, lanes] * moved
        pre_ref[:, lanes] = total
        return total * sigmoid(total)

    write_rows = convolve(slice(IP, IP + N))
    read_rows = convolve(slice(IP + N, CP))
    _, timestep, decay = steps_of(pt_ref[:, 2 * N : SMALL], heads)
    sums_col, sums_row = block_sums(decay)
    affinity, crossing = [], [None]
    for b in range(blocks):
        span = slice(b * BLOCK, (b + 1) * BLOCK)
        affinity.append(mm(read_rows[span], write_rows[span], COLS_COLS))
        if b:
            before = slice((b - 1) * BLOCK, b * BLOCK)
            crossing.append(
                jnp.where(
                    across(seg_col, seg_row, b), mm(read_rows[span], write_rows[before], COLS_COLS), 0.0
                ).astype(LOW)
            )
    seen = [visible_in(seg_col, seg_row, b) for b in range(blocks)]
    lanes_low = lax.broadcasted_iota(jnp.int32, (1, PAIR), 1) < P_SIZE
    entry = [jnp.exp(c) for c in sums_col]
    tail = [jnp.exp(c[BLOCK - 1 : BLOCK, :] - c) for c in sums_col]
    for pair in range(HP // 2):
        lanes = slice(pair * PAIR, (pair + 1) * PAIR)
        inputs = convolve(lanes)
        scaled = inputs * per_pair(timestep, pair, lanes_low)
        skip = jnp.where(lanes_low, heads[2:3, 2 * pair : 2 * pair + 1], heads[2:3, 2 * pair + 1 : 2 * pair + 2])
        for b in range(blocks):
            span = slice(b * BLOCK, (b + 1) * BLOCK)
            scores = []
            for h in (2 * pair, 2 * pair + 1):
                spread = column(sums_col[b], h) - sums_row[b][h : h + 1, :]
                scores.append((affinity[b] * jnp.exp(jnp.where(seen[b], spread, MASKED))).astype(LOW))
            here = scaled[span]
            stacked = jnp.concatenate(
                [jnp.where(lanes_low, here, 0.0), jnp.where(lanes_low, 0.0, here)], axis=0
            )
            out = mm(jnp.concatenate(scores, axis=1), stacked)
            if b:
                before = slice((b - 1) * BLOCK, b * BLOCK)
                weighted = scaled[before] * per_pair(tail[b - 1], pair, lanes_low)
                out = out + per_pair(entry[b], pair, lanes_low) * mm(crossing[b], weighted)
            y_ref[span, lanes] = out + skip * inputs[span]


def backward_kernel(
    px_ref,
    pt_ref,
    pre_ref,
    y_ref,
    dy_ref,
    taps_ref,
    heads_ref,
    segc_ref,
    segr_ref,
    mask_ref,
    dx_ref,
    dt_ref,
    dtaps_ref,
    dheads_ref,
):
    tokens = px_ref.shape[0]
    blocks = tokens // BLOCK
    heads = heads_ref[...]
    seg_col, seg_row = segc_ref[...], segr_ref[...]
    mask = mask_ref[...]
    taps = taps_ref[...]

    def activate(lanes):
        pre = pre_ref[:, lanes]
        sig = sigmoid(pre)
        return pre * sig, sig * (1.0 + pre * (1.0 - sig))

    def unconvolve(lanes, grad):
        source = source_of(px_ref, pt_ref, lanes)
        result = taps[CK - 1 : CK, lanes] * grad
        dtaps_ref[CK : CK + 1, lanes] = jnp.sum(grad, axis=0, keepdims=True)
        dtaps_ref[CK - 1 : CK, lanes] = jnp.sum(grad * source, axis=0, keepdims=True)
        for back in range(1, CK):
            at = CK - 1 - back
            kept = grad * column(mask, back)
            moved = pltpu.roll(kept, tokens - back, 0)
            dtaps_ref[at : at + 1, lanes] = jnp.sum(moved * source, axis=0, keepdims=True)
            result = result + taps[at : at + 1, lanes] * moved
        if lanes.start < IP:
            dx_ref[:, lanes] = result.astype(LOW)
        else:
            dt_ref[:, lanes.start - IP : lanes.stop - IP] = result.astype(LOW)

    write_rows, write_slope = activate(slice(IP, IP + N))
    read_rows, read_slope = activate(slice(IP + N, CP))
    raw, timestep, decay = steps_of(pt_ref[:, 2 * N : SMALL], heads)
    sums_col, sums_row = block_sums(decay)
    affinity, crossing = [], [None]
    for b in range(blocks):
        span = slice(b * BLOCK, (b + 1) * BLOCK)
        affinity.append(mm(read_rows[span], write_rows[span], COLS_COLS))
        if b:
            before = slice((b - 1) * BLOCK, b * BLOCK)
            crossing.append(
                jnp.where(
                    across(seg_col, seg_row, b), mm(read_rows[span], write_rows[before], COLS_COLS), 0.0
                ).astype(LOW)
            )
    seen = [visible_in(seg_col, seg_row, b) for b in range(blocks)]
    lanes_low = lax.broadcasted_iota(jnp.int32, (1, PAIR), 1) < P_SIZE
    head_lane = lax.broadcasted_iota(jnp.int32, (1, HP), 1)
    entry = [jnp.exp(c) for c in sums_col]
    tail = [jnp.exp(c[BLOCK - 1 : BLOCK, :] - c) for c in sums_col]
    d_affinity = [jnp.zeros((BLOCK, BLOCK), F32) for _ in range(blocks)]
    d_crossing = [jnp.zeros((BLOCK, BLOCK), F32) for _ in range(blocks)]
    d_sums = [jnp.zeros((BLOCK, HP), F32) for _ in range(blocks)]
    d_steps = [jnp.zeros((BLOCK, HP), F32) for _ in range(blocks)]
    d_skip = jnp.zeros((1, HP), F32)

    def spread_heads(values, pair):
        low = jnp.sum(jnp.where(lanes_low, values, 0.0), axis=1, keepdims=True)
        high = jnp.sum(jnp.where(lanes_low, 0.0, values), axis=1, keepdims=True)
        return jnp.where(head_lane == 2 * pair, low, 0.0) + jnp.where(
            head_lane == 2 * pair + 1, high, 0.0
        )

    for pair in range(HP // 2):
        lanes = slice(pair * PAIR, (pair + 1) * PAIR)
        inputs, slope = activate(lanes)
        step = per_pair(timestep, pair, lanes_low)
        scaled = inputs * step
        skip = jnp.where(lanes_low, heads[2:3, 2 * pair : 2 * pair + 1], heads[2:3, 2 * pair + 1 : 2 * pair + 2])
        y = y_ref[:, lanes]
        d_y = dy_ref[:, lanes]
        d_skip = d_skip + jnp.sum(spread_heads(d_y * inputs, pair), axis=0, keepdims=True)
        d_y_low = d_y.astype(LOW)
        d_y_round = d_y_low.astype(F32)
        scan = y - skip * inputs
        scaled_low = scaled.astype(LOW)
        scaled_round = scaled_low.astype(F32)
        d_scaled = [None] * blocks
        for b in range(blocks):
            span = slice(b * BLOCK, (b + 1) * BLOCK)
            grads, here = d_y_round[span], scaled_low[span]
            stacked = jnp.concatenate(
                [jnp.where(lanes_low, grads, 0.0), jnp.where(lanes_low, 0.0, grads)], axis=0
            ).astype(LOW)
            d_scores = mm(stacked, here, COLS_COLS)
            scores = []
            for i, h in enumerate((2 * pair, 2 * pair + 1)):
                spread = column(sums_col[b], h) - sums_row[b][h : h + 1, :]
                fade = jnp.exp(jnp.where(seen[b], spread, MASKED))
                d_affinity[b] = d_affinity[b] + d_scores[i * BLOCK : (i + 1) * BLOCK] * fade
                scores.append((affinity[b] * fade).astype(LOW))
            d_here = mm(jnp.concatenate(scores, axis=0), stacked, ROWS_COLS)
            d_scaled[b] = d_here if d_scaled[b] is None else d_scaled[b] + d_here
            d_sums[b] = d_sums[b] + spread_heads(grads * scan[span], pair)
            if b:
                before = slice((b - 1) * BLOCK, b * BLOCK)
                tail_here = per_pair(tail[b - 1], pair, lanes_low)
                weighted = (scaled[before] * tail_here).astype(LOW)
                incoming = (d_y[span] * per_pair(entry[b], pair, lanes_low)).astype(LOW)
                d_weighted = mm(crossing[b], incoming, ROWS_COLS)
                d_crossing[b] = d_crossing[b] + mm(incoming, weighted, COLS_COLS)
                d_scaled[b - 1] = d_scaled[b - 1] + tail_here * d_weighted
        for b in range(blocks):
            span = slice(b * BLOCK, (b + 1) * BLOCK)
            d_sums[b] = d_sums[b] - spread_heads(scaled_round[span] * d_scaled[b], pair)
            d_steps[b] = d_steps[b] + spread_heads(inputs[span] * d_scaled[b], pair)
        d_inputs = jnp.concatenate(d_scaled, axis=0) * step + skip * d_y
        unconvolve(lanes, d_inputs * slope)

    ones = lower_ones(BLOCK)
    d_write = [jnp.zeros((BLOCK, N), F32) for _ in range(blocks)]
    d_read = [None] * blocks
    d_decay = [None] * blocks
    later = jnp.zeros((1, HP), F32)
    for b in range(blocks):
        span = slice(b * BLOCK, (b + 1) * BLOCK)
        d_read[b] = mm(d_affinity[b], write_rows[span])
        d_write[b] = d_write[b] + mm(d_affinity[b], read_rows[span], ROWS_COLS)
        if b:
            before = slice((b - 1) * BLOCK, b * BLOCK)
            kept = jnp.where(across(seg_col, seg_row, b), d_crossing[b], 0.0)
            d_read[b] = d_read[b] + mm(kept, write_rows[before])
            d_write[b - 1] = d_write[b - 1] + mm(kept, read_rows[span], ROWS_COLS)
    for b in reversed(range(blocks)):
        d_decay[b] = exact_mm(ones, d_sums[b], ROWS_COLS) + later
        later = later + jnp.sum(d_sums[b], axis=0, keepdims=True)
    unconvolve(slice(IP, IP + N), jnp.concatenate(d_write, axis=0) * write_slope)
    unconvolve(slice(IP + N, CP), jnp.concatenate(d_read, axis=0) * read_slope)
    d_decay = jnp.concatenate(d_decay, axis=0)
    d_raw = (jnp.concatenate(d_steps, axis=0) - d_decay * jnp.exp(heads[0:1, :])) * sigmoid(raw)
    padding = jnp.zeros((tokens, WT - SMALL), LOW)
    dt_ref[:, 2 * N :] = jnp.concatenate([d_raw.astype(LOW), padding], axis=1)
    dheads_ref[0:1, :] = jnp.sum(d_decay * decay, axis=0, keepdims=True)
    dheads_ref[1:2, :] = jnp.sum(d_raw, axis=0, keepdims=True)
    dheads_ref[2:3, :] = d_skip


def call(kernel, outs, *args):
    return pl.pallas_call(
        kernel,
        out_shape=[jax.ShapeDtypeStruct(shape, kind) for shape, kind in outs],
        interpret=INTERPRET,
    )(*args)


def swap(x, by):
    return lax.ppermute(x, "dp", [(i, i ^ by) for i in range(lax.axis_size("dp"))])


def after(x, *earlier):
    return lax.optimization_barrier((x,) + earlier)[0]


def place_kernel(dims, count, at_ref, *refs):
    left_ref = None
    if dims is not None:
        left_ref, refs = refs[0], refs[1:]
    sources, outs = refs[:8], refs[8 : 8 + count]
    chip = at_ref[0]
    rows = sources[0].shape[0] // 2
    for n, source in enumerate(sources):
        for i in range(2):
            k, j = n // 2, n % 2 * 2 + i
            to = pl.multiple_of((chip ^ (4 * j + k)) * rows, rows)
            start = 0
            for out_ref in outs:
                stop = start + out_ref.shape[1]
                out_ref[pl.ds(to, rows), :] = source[i * rows : (i + 1) * rows, start:stop]
                start = stop
    if dims is not None:
        refs[8 + count][...] = mm(left_ref[...], outs[0][...], dims)


def put(sources, left=None, dims=None, widths=None):
    rows = sum(v.shape[0] for v in sources)
    widths = widths or (sources[0].shape[1],)
    outs = [jax.ShapeDtypeStruct((rows, width), LOW) for width in widths]
    extra = []
    if left is not None:
        extra = [left]
        columns = widths[0] if dims[0][1] == (0,) else rows
        outs.append(jax.ShapeDtypeStruct((left.shape[0], columns), F32))
    return pl.pallas_call(
        functools.partial(place_kernel, dims, len(widths)),
        out_shape=outs,
        in_specs=[pl.BlockSpec(memory_space=pltpu.SMEM)] + [pl.BlockSpec()] * (len(extra) + len(sources)),
        interpret=INTERPRET,
    )(lax.axis_index("dp")[None].astype(jnp.int32), *extra, *sources)


def stack_kernel(*refs):
    *sources, top_ref, low_ref = refs
    rows = sources[0].shape[0]
    for n, source in enumerate(sources):
        (top_ref if n < 2 else low_ref)[(n % 2) * rows : (n % 2 + 1) * rows, :] = source[...]


def gather_depth(x, *earlier):
    x = after(x, *earlier) if earlier else x
    return [x] + [swap(x, 4 * j) for j in range(1, 4)]


def gather_plane(parts, *earlier):
    if earlier:
        parts = lax.optimization_barrier(tuple(parts) + earlier)[:4]
    rows, width = parts[0].shape
    top, low = call(stack_kernel, [((2 * rows, width), LOW)] * 2, *parts)
    top_x, top_y, low_x, low_y = swap(top, 1), swap(top, 2), swap(low, 1), swap(low, 2)
    far_top, far_low = swap(top_y, 1), swap(low_x, 2)
    return [top, low, top_x, low_x, top_y, low_y, far_top, far_low]


def add(first, *others):
    total = first.astype(F32)
    for v in others:
        total = total + v.astype(F32)
    return total


def blocks_kernel(at_ref, left_ref, *refs):
    *rights, own_ref, x_ref, y_ref, high_ref, low_ref, whole_ref = refs
    start = 0
    left = left_ref[...]
    for right in rights:
        if right.dtype == LOW:
            width = right.shape[1]
            whole_ref[:, start : start + width] = mm(left, right[...], ROWS_COLS)
            start += width
        else:
            whole_ref[:, start - right.shape[1] : start] += right[...]
    plane = at_ref[0] % 4
    rows = own_ref.shape[1]
    for z in range(4):
        for k, (ref, at) in enumerate(
            ((own_ref, z), (x_ref, z), (y_ref, z), (high_ref if z < 2 else low_ref, z % 2))
        ):
            source = pl.multiple_of((4 * z + (plane ^ k)) * rows, rows)
            ref[at] = whole_ref[pl.ds(source, rows), :].astype(LOW)


def blocks_of(left, *rights):
    rows = left.shape[1] // 16
    width = sum(v.shape[1] for v in rights if v.dtype == LOW)
    return pl.pallas_call(
        blocks_kernel,
        out_shape=[jax.ShapeDtypeStruct((n, rows, width), LOW) for n in (4, 4, 4, 2, 2)],
        in_specs=[pl.BlockSpec(memory_space=pltpu.SMEM)] + [pl.BlockSpec()] * (1 + len(rights)),
        scratch_shapes=[pltpu.VMEM((16 * rows, width), F32)],
        interpret=INTERPRET,
    )(lax.axis_index("dp")[None].astype(jnp.int32), left, *rights)


def scatter_far(blocks):
    return swap(blocks[3], 1), swap(blocks[4], 2)


def near_kernel(x_ref, y_ref, from_x_ref, from_y_ref, *refs):
    *notes, to_x_ref, to_y_ref = refs
    to_x_ref[0:2] = x_ref[0:2]
    to_x_ref[2:4] = (x_ref[2:4].astype(F32) + from_y_ref[...].astype(F32)).astype(LOW)
    to_y_ref[0:2] = (y_ref[0:2].astype(F32) + from_x_ref[...].astype(F32)).astype(LOW)
    to_y_ref[2:4] = y_ref[2:4]
    if notes:
        at = to_y_ref.shape[2] - 128
        lanes = note_lanes(128)
        for z in range(4):
            to_y_ref[z, :, at:] = jnp.where(lanes, notes[0][...], to_y_ref[z, :, at:])


def scatter_near(blocks, arrived, notes=()):
    _, near_x, near_y, _, _ = blocks
    kind = (near_x.shape, LOW)
    to_x, to_y = call(near_kernel, [kind, kind], near_x, near_y, *arrived, *notes)
    return swap(to_x, 1), swap(to_y, 2)


def depth_kernel(at_ref, own_ref, from_x_ref, from_y_ref, *refs):
    *notes, layer_ref, one_ref, two_ref, three_ref = refs
    depth = at_ref[0] // 4
    for j, ref in enumerate((layer_ref, one_ref, two_ref, three_ref)):
        z = depth ^ j
        total = own_ref[z].astype(F32) + from_x_ref[z].astype(F32) + from_y_ref[z].astype(F32)
        ref[...] = total.astype(ref.dtype)
        if notes:
            at = ref.shape[1] - 128
            ref[:, at:] = jnp.where(note_lanes(128), notes[0][...].astype(ref.dtype), ref[:, at:])


def scatter_depth(blocks, arrived, notes=()):
    _, rows, width = blocks[0].shape
    own, *layers = pl.pallas_call(
        depth_kernel,
        out_shape=[jax.ShapeDtypeStruct((rows, width), kind) for kind in (F32, LOW, LOW, LOW)],
        in_specs=[pl.BlockSpec(memory_space=pltpu.SMEM)] + [pl.BlockSpec()] * (3 + len(notes)),
        interpret=INTERPRET,
    )(lax.axis_index("dp")[None].astype(jnp.int32), blocks[0], *arrived, *notes)
    return (own,) + tuple(swap(v, 4 * (j + 1)) for j, v in enumerate(layers))


def note_lanes(width):
    lane = lax.broadcasted_iota(jnp.int32, (1, width), 1)
    return lane >= width - NOTE_WIDTH


def write_notes(values, rows):
    parts, rest = [], values
    for _ in range(3):
        part = lax.reduce_precision(rest, 8, 7)
        parts.append(part)
        rest = rest - part
    tile = jnp.concatenate(parts, axis=0).astype(LOW)
    return jnp.pad(tile, ((0, rows - tile.shape[0]), (128 - NOTE_WIDTH, 0)))


def read_notes(layer):
    parts = layer[:9, layer.shape[1] - NOTE_WIDTH :].astype(F32)
    return parts[0:3] + parts[3:6] + parts[6:9]


def tail_kernel(place_ref, taps_ref, gate_ref, norm_ref, notes_ref, out_ref, full_ref, rows_ref):
    first = place_ref[0] == 0
    none = jnp.zeros((8, P_SIZE), F32)
    for pair in range(HP // 2):
        v = taps_ref[:, pair * PAIR : (pair + 1) * PAIR]
        a, b = v[:, :P_SIZE], v[:, P_SIZE:]
        even = jnp.concatenate([a, none, b, none], axis=1)
        odd = jnp.concatenate([none, a, none, b], axis=1)
        full_ref[:, pair * 2 * PAIR : (pair + 1) * 2 * PAIR] = jnp.where(first, even, odd)
    full_ref[:, DI:] = taps_ref[:, IP:]
    rows_ref[...] = jnp.zeros(rows_ref.shape, F32)
    rows_ref[0:1, :] = norm_ref[...]
    rows_ref[1:2, :] = gate_ref[...]
    span = rows_ref.shape[1] // 32
    each = CONV // 32
    taps = CK + 1
    for core in range(32):
        for g in range(-(-each // span)):
            width = min(span, each - g * span)
            source = core * each + g * span
            rows_ref[2 + taps * g : 2 + taps * (g + 1), core * span : core * span + width] = full_ref[
                0:taps, source : source + width
            ]
    row = lax.broadcasted_iota(jnp.int32, (32, 128), 0)
    col = lax.broadcasted_iota(jnp.int32, (32, 128), 1)
    columns = mm(rows_ref[...], col == row + HP, ROWS_COLS)
    height = notes_ref.shape[0]
    for block in range(16):
        at = slice(block * height, (block + 1) * height)
        out_ref[at, :] = columns[at, :] + notes_ref[...].astype(F32)


def tail_columns(d_taps, d_gate, d_norm, notes):
    rows = d_norm.shape[1]
    return pl.pallas_call(
        tail_kernel,
        out_shape=jax.ShapeDtypeStruct((rows, 128), F32),
        in_specs=[pl.BlockSpec(memory_space=pltpu.SMEM)] + [pl.BlockSpec()] * 4,
        scratch_shapes=[pltpu.VMEM((8, CONV), F32), pltpu.VMEM((32, rows), F32)],
        interpret=INTERPRET,
    )(lax.axis_index("seq")[None].astype(jnp.int32), d_taps, d_gate, d_norm, notes)


def split_kernel(place_ref, w_ref, tail_ref, mine_ref, other_ref):
    first = place_ref[0] == 0
    shared = w_ref[:, 2 * DI : DI + CONV].astype(LOW)
    for ref, p in ((mine_ref, 0), (other_ref, 1)):
        ref[:, : 2 * N] = shared
        ref[:, 2 * N : WT] = tail_ref[p]
    for group in range(IP // 128):
        for base, to in ((DI, WT), (0, WT + IP)):
            at = base + 256 * group
            block = w_ref[:, at : at + 256]
            even = jnp.concatenate([block[:, 0:64], block[:, 128:192]], axis=1)
            odd = jnp.concatenate([block[:, 64:128], block[:, 192:256]], axis=1)
            lanes = slice(to + 128 * group, to + 128 * (group + 1))
            mine_ref[:, lanes] = jnp.where(first, even, odd).astype(LOW)
            other_ref[:, lanes] = jnp.where(first, odd, even).astype(LOW)


def small_width(rows):
    per_core = CONV // (DI // P_SIZE)
    return per_core * (CK + 1), -(-(per_core * (CK + 1)) // rows)


def payloads(norm_gain, in_weight, conv_weight, gate_gain):
    place = lax.axis_index("seq")
    first = place == 0
    rows = in_weight.shape[0]
    values, width = small_width(rows)
    steps = planes_of(in_weight[:, DI + CONV :], 1)
    conv_flat = jnp.pad(conv_weight.reshape(-1), (0, rows * width - values)).reshape(rows, width)
    gate_two = gate_gain.reshape(2, rows).T
    zero = jnp.zeros_like(gate_two)
    fill = jnp.zeros((rows, WT - SMALL - 3 - width), F32)

    def tail(step, gate):
        return jnp.concatenate([step, norm_gain[:, None], gate, conv_flat, fill], axis=1)

    tails = jnp.stack(
        [
            tail(jnp.where(first, steps[0], steps[1]), gate_two),
            tail(jnp.where(first, steps[1], steps[0]), zero),
        ]
    ).astype(LOW)
    shape = jax.ShapeDtypeStruct((rows, WT + 2 * IP), LOW)
    mine, send = pl.pallas_call(
        split_kernel,
        out_shape=[shape, shape],
        in_specs=[pl.BlockSpec(memory_space=pltpu.SMEM), pl.BlockSpec(), pl.BlockSpec()],
        interpret=INTERPRET,
    )(place[None].astype(jnp.int32), in_weight, tails)
    other = sibling(send)
    chip = jnp.concatenate([jnp.where(first, mine, other), jnp.where(first, other, mine)], axis=0)
    return chip[:, : WT + IP], chip[:, WT + IP :]


def unpack(w_t):
    chips = 16
    rows = w_t.shape[0] // (2 * chips)
    values, width = small_width(rows)
    small = w_t[:, SMALL : SMALL + 3 + width].astype(F32)
    norm = small[:, 0]
    gate = small[:, 1:3].reshape(chips, 2, rows, 2).sum(1).transpose(0, 2, 1).reshape(-1)
    conv = small[:, 3:].reshape(2 * chips, rows * width)[:, :values].reshape(CONV, CK + 1).T
    return norm, gate, plane_taps(conv)


def plane_taps(conv):
    x = planes_of(conv[:, :DI], 1)
    x = jnp.where(lax.axis_index("seq") == 0, x[0], x[1])
    taps = jnp.concatenate([x, conv[:, DI:]], axis=1)
    return jnp.pad(taps, ((0, 8 - taps.shape[0]), (0, 0)))


def all_taps(d_taps):
    d_taps = d_taps[: CK + 1]
    x, shared = d_taps[:, :IP], d_taps[:, IP:]
    first = lax.axis_index("seq") == 0
    none = jnp.zeros_like(x)
    even, odd = jnp.where(first, x, none), jnp.where(first, none, x)
    return jnp.concatenate([interleave(even, odd, 1), shared], axis=1).T


def all_heads(d_heads):
    first = lax.axis_index("seq") == 0
    none = jnp.zeros_like(d_heads)
    return interleave(jnp.where(first, d_heads, none), jnp.where(first, none, d_heads), 1)


def rows_back(chip_rows):
    first = lax.axis_index("seq") == 0
    rows = chip_rows.shape[0] // 2
    low, high = chip_rows[:rows], chip_rows[rows:]
    keep = jnp.where(first, low, high)
    other = sibling(jnp.where(first, high, low))
    return jnp.where(first, keep, other), jnp.where(first, other, keep)


def update_kernel(
    z_even, z_odd, a_even, a_odd, weight, first, second, grad_ref, weight_ref, first_ref, second_ref
):
    def update(at, grad):
        lanes = slice(at, at + grad.shape[1])
        grad_ref[:, lanes] = grad
        new = adamw(weight[:, lanes], grad, first[:, lanes], second[:, lanes])
        weight_ref[:, lanes], first_ref[:, lanes], second_ref[:, lanes] = new

    for base, even, odd in ((0, z_even, z_odd), (DI, a_even, a_odd)):
        for group in range(IP // 128):
            e = even[:, 128 * group : 128 * (group + 1)]
            o = odd[:, 128 * group : 128 * (group + 1)]
            pieces = [e[:, :P_SIZE], o[:, :P_SIZE], e[:, P_SIZE:], o[:, P_SIZE:]]
            update(base + 256 * group, jnp.concatenate(pieces, axis=1))
    shared = slice(IP, IP + 2 * N)
    update(2 * DI, a_even[:, shared] + a_odd[:, shared])
    at = IP + 2 * N
    e, o = a_even[:, at : at + 128], a_odd[:, at : at + 128]
    row = lax.broadcasted_iota(jnp.int32, (128, H), 0)
    col = lax.broadcasted_iota(jnp.int32, (128, H), 1)
    update(DI + CONV, exact_mm(e, (col == 2 * row).astype(F32)) + exact_mm(o, (col == 2 * row + 1).astype(F32)))


def fetch_any(norm_low, in_low, conv_low, gate_low, out_low):
    norm, w_in, conv, gate, w_out = (
        lax.all_gather(v, ("dp", "seq"), axis=0, tiled=True)
        for v in (norm_low, in_low, conv_low, gate_low, out_low)
    )
    first = lax.axis_index("seq") == 0

    def mine(v, axis):
        parts = planes_of(v, axis)
        return jnp.where(first, parts[0], parts[1])

    w_t = jnp.concatenate(
        [
            w_in[:, 2 * DI : DI + CONV],
            mine(w_in[:, DI + CONV :], 1),
            jnp.zeros((w_in.shape[0], WT - SMALL), LOW),
        ],
        axis=1,
    )
    return (
        w_t,
        mine(w_in[:, DI : 2 * DI], 1),
        mine(w_in[:, :DI], 1),
        mine(w_out, 0),
        norm.astype(F32),
        mine(gate, 0).astype(F32),
        plane_taps(conv.astype(F32).T),
    )


def embed(v, axis):
    first = lax.axis_index("seq") == 0
    none = jnp.zeros_like(v)
    return interleave(jnp.where(first, v, none), jnp.where(first, none, v), axis)


def return_any(d_t, d_x, d_z, d_norm, d_gate, d_taps, d_out):
    def total(v):
        return lax.psum_scatter(v, ("dp", "seq"), scatter_dimension=0, tiled=True)

    d_in = jnp.concatenate(
        [embed(d_z, 1), embed(d_x, 1), d_t[:, : 2 * N], embed(d_t[:, 2 * N : SMALL], 1)], axis=1
    )
    return (
        total(d_in.astype(LOW)).astype(F32),
        total(d_norm),
        total(all_taps(d_taps)),
        total(embed(d_gate, 0)),
        total(embed(d_out, 0).astype(LOW)).astype(F32),
    )


def on_device(
    resid,
    segment_ids,
    cotangent,
    norm_gain,
    in_weight,
    conv_weight,
    gate_gain,
    out_weight,
    head_params,
    first_norm,
    first_in,
    first_conv,
    first_gate,
    first_out,
    first_head,
    second_norm,
    second_in,
    second_conv,
    second_gate,
    second_out,
    second_head,
):
    place = lax.axis_index("seq")
    local_rows = resid[0]
    cot_rows = cotangent[0]
    segments = segment_ids[0]
    tokens = segments.shape[0]
    one_head = out_weight.shape[0] == P_SIZE and lax.axis_size("dp") == 16
    all_rows = both_halves(local_rows)
    cot_half = both_halves(cot_rows.astype(LOW))

    def inverse_rms(values):
        return lax.rsqrt(jnp.mean(values * values, axis=-1, keepdims=True) + NORM_EPS)

    if one_head:
        low_a, low_z = payloads(norm_gain, in_weight, conv_weight, gate_gain)
        deep_a = gather_depth(low_a)
        segments, head_params_here = lax.optimization_barrier((segments, head_params) + tuple(deep_a[1:]))[:2]
    else:
        head_params_here = head_params
    heads = planes_of(head_params_here, 1)
    heads = jnp.pad(jnp.where(place == 0, heads[0], heads[1]), ((0, 5), (0, 0)))
    seg_col, seg_row = segments[:, None], segments[None, :]
    masks = [jnp.ones((tokens,), F32)]
    for back in range(1, CK):
        same = (segments[back:] == segments[:-back]).astype(F32)
        masks.append(jnp.concatenate([jnp.zeros((back,), F32), same]))
    mask = jnp.stack(masks, axis=1)

    def normed_by(norm):
        return (all_rows * inverse_rms(all_rows) * norm).astype(LOW)

    if one_head:
        parts_a = gather_plane(deep_a)
        deep_z = gather_depth(low_z, *deep_a[1:])
        parts_z = gather_plane(deep_z, *parts_a[2:6])
        deep_out = gather_depth(out_weight.astype(LOW), *deep_z[1:])
        parts_out = gather_plane(deep_out, *parts_z[2:6])
        w_t, w_x = put(parts_a, widths=(WT, IP))
        norm, gate, taps = unpack(w_t)
        normed_half = normed_by(norm)
        proj_t = mm(normed_half, w_t)
        proj_x = mm(normed_half, w_x)
        w_z, z = put(parts_z, normed_half, NORMAL)
        w_out, grad_mixed = put(parts_out, cot_half, COLS_COLS)
    else:
        lows = [v.astype(LOW) for v in (norm_gain, in_weight, conv_weight, gate_gain, out_weight)]
        w_t, w_x, w_z, w_out, norm, gate, taps = fetch_any(*lows)
        normed_half = normed_by(norm)
        proj_t, proj_x, z = (mm(normed_half, w) for w in (w_t, w_x, w_z))
        grad_mixed = mm(cot_half, w_out, COLS_COLS)
    pre, y = call(
        forward_kernel,
        [((tokens, CP), F32), ((tokens, IP), F32)],
        proj_x,
        proj_t,
        taps,
        heads,
        seg_col,
        seg_row,
        mask,
    )
    sig = sigmoid(z)
    silu = z * sig
    gated = y * silu
    partial = jnp.stack(
        [jnp.sum(gated * gated, axis=1), jnp.sum(grad_mixed * gate * gated, axis=1)], axis=0
    )
    both = partial + sibling(partial)
    scale = lax.rsqrt(both[0] / DI + NORM_EPS)
    pull = (scale * scale * scale * both[1] / DI)[:, None]
    scale = scale[:, None]
    mixed_half = (gated * scale * gate).astype(LOW)
    if one_head:
        blocks_out = blocks_of(mixed_half, cot_half)
        far_out = scatter_far(blocks_out)
        scale = after(scale, *blocks_out[3:])
    d_gated = scale * (grad_mixed * gate) - gated * pull
    d_z = (d_gated * y * (sig * (1.0 + z * (1.0 - sig)))).astype(LOW)
    d_y = d_gated * silu
    d_gate = jnp.sum(grad_mixed * gated * scale, axis=0)
    if one_head:
        blocks_z = blocks_of(normed_half, d_z)
        far_z = scatter_far(blocks_z)
        near_out = scatter_near(blocks_out, far_out)
        near_z = scatter_near(blocks_z, far_z)
        d_y = after(d_y, *far_out, *far_z)
    d_proj_x, d_proj_t, d_taps, d_heads = call(
        backward_kernel,
        [((tokens, IP), LOW), ((tokens, WT), LOW), ((8, CP), F32), ((3, HP), F32)],
        proj_x,
        proj_t,
        pre,
        y,
        d_y,
        taps,
        heads,
        seg_col,
        seg_row,
        mask,
    )
    partial_normed = mm(d_proj_x, w_x, COLS_COLS) + mm(d_proj_t, w_t, COLS_COLS) + mm(d_z, w_z, COLS_COLS)
    d_norm = jnp.sum(partial_normed * all_rows * inverse_rms(all_rows), axis=0)
    if one_head:
        rows = in_weight.shape[0]
        notes = write_notes(d_heads, 2 * rows)
        small = tail_columns(d_taps, d_gate[None], d_norm[None], notes)
        blocks_a = blocks_of(normed_half, d_proj_x, d_proj_t, small)
        far_a = scatter_far(blocks_a)
        terms_out = scatter_depth(blocks_out, near_out)
        heads_here = read_notes(notes) + read_notes(far_a[0][0])
        notes = write_notes(heads_here, 2 * rows)
        near_a = scatter_near(blocks_a, far_a, (notes,))
        terms_z = scatter_depth(blocks_z, near_z)
        heads_here = read_notes(notes) + read_notes(near_a[1][0])
        terms_a = scatter_depth(blocks_a, near_a, (write_notes(heads_here, 2 * rows),))
        partial_normed, mixed_half, *terms = lax.optimization_barrier(
            (partial_normed, mixed_half) + terms_out[1:] + terms_z[1:] + near_a
        )[:8]
        shard_out = add(terms_out[0], *terms[:3])
        back_z = rows_back(add(terms_z[0], *terms[3:]))
    else:
        d_in_t, d_in_x, d_in_z = (mm(normed_half, v, ROWS_COLS) for v in (d_proj_t, d_proj_x, d_z))
        d_out = mm(mixed_half, cot_half, ROWS_COLS)
        shard_in, shard_norm, shard_conv, shard_gate, shard_out = return_any(
            d_in_t, d_in_x, d_in_z, d_norm, d_gate, d_taps, d_out
        )
        head_total = lax.psum(all_heads(d_heads), ("dp", "seq"))

    result = local_rows + own_half(mm(mixed_half, w_out))
    grad_normed = own_half(partial_normed)
    inv = inverse_rms(local_rows)
    weighted = grad_normed * norm
    dots = jnp.mean(weighted * local_rows, axis=-1, keepdims=True)
    grad_input = cot_rows + inv * weighted - local_rows * (inv * inv * inv * dots)
    updated_out = adamw(out_weight, shard_out, first_out, second_out)
    if one_head:
        early = (result, grad_input, shard_out, *updated_out, *back_z)
        late = lax.optimization_barrier(early + terms_a)
        result, grad_input, shard_out, *updated_out = late[:6]
        back_z, terms_a = late[6:8], late[8:]
        chip_a = add(*terms_a)
        depth = lax.axis_index("dp") // 4
        every = jnp.stack([read_notes(v) for v in terms_a])
        every = [lax.dynamic_index_in_dim(every, depth ^ j, 0, keepdims=False) for j in range(4)]
        d_heads = every[0] + every[1] + every[2] + every[3]
        other = sibling(d_heads)
        first = place == 0
        head_total = interleave(jnp.where(first, d_heads, other), jnp.where(first, other, d_heads), 1)
        back_a = rows_back(chip_a)
        tail = back_a[0][:, IP + 2 * N :] + back_a[1][:, IP + 2 * N :]
        shape = (in_weight.shape, F32)
        new_in = call(update_kernel, [shape] * 4, *back_z, *back_a, in_weight, first_in, second_in)
        shard_in = new_in[0]
        small = tail[:, HP:]
        shard_norm = small[:, 0]
        shard_gate = chip_a[:, IP + SMALL + 1]
        groups = -(-conv_weight.shape[0] // rows)
        conv = small[:, 2 : 2 + groups * (CK + 1)].reshape(rows, groups, CK + 1).transpose(1, 0, 2)
        shard_conv = conv.reshape(-1, CK + 1)[: conv_weight.shape[0]]
        updated_in = new_in[1:]
    else:
        updated_in = adamw(in_weight, shard_in, first_in, second_in)
    new_norm, new_first_norm, new_second_norm = adamw(
        norm_gain, shard_norm, first_norm, second_norm
    )
    new_in, new_first_in, new_second_in = updated_in
    new_conv, new_first_conv, new_second_conv = adamw(
        conv_weight, shard_conv, first_conv, second_conv
    )
    new_gate, new_first_gate, new_second_gate = adamw(
        gate_gain, shard_gate, first_gate, second_gate
    )
    new_out, new_first_out, new_second_out = updated_out
    new_head, new_first_head, new_second_head = adamw(
        head_params, head_total, first_head, second_head
    )
    return (
        result[None],
        grad_input[None],
        shard_norm,
        shard_in,
        shard_conv,
        shard_gate,
        shard_out,
        head_total,
        new_norm,
        new_in,
        new_conv,
        new_gate,
        new_out,
        new_head,
        new_first_norm,
        new_first_in,
        new_first_conv,
        new_first_gate,
        new_first_out,
        new_first_head,
        new_second_norm,
        new_second_in,
        new_second_conv,
        new_second_gate,
        new_second_out,
        new_second_head,
    )


def solution(mesh):
    step = whole_step(mesh)
    return step


def whole_step(mesh):
    rows = P(("dp", "seq"))
    wide = P(("dp", "seq"), None)
    tokens = P("dp", "seq", None)
    weights = (rows, wide, wide, rows, wide, P())

    return jax.shard_map(
        on_device,
        mesh=mesh,
        in_specs=(tokens, P("dp", None), tokens) + weights * 3,
        out_specs=(tokens, tokens) + weights_out() * 4,
        check_vma=False,
    )


def weights_out():
    rows = P(("dp", "seq"))
    wide = P(("dp", "seq"), None)
    return (rows, wide, wide, rows, wide, P())
```

```python
import functools

import jax
import jax.numpy as jnp
from jax import lax
from jax.experimental import pallas as pl
from jax.experimental.pallas import tpu as pltpu
from jax.sharding import PartitionSpec as P


H = 32
P_SIZE = 64
N = 128
CK = 4
BLOCK = 128
STEP = 4
DI = 2048
CONV = 2304


NORM_EPS = 1e-05
LEARNING_RATE = 0.02
BETA_FIRST = 0.9
BETA_SECOND = 0.95
ADAM_EPS = 1e-08
WEIGHT_DECAY = 0.1
HIGHEST = lax.Precision.HIGHEST
MASKED = -1e30
INTERPRET = False

PLANES = 2
HP = H // PLANES
IP = HP * P_SIZE
CP = IP + 2 * N
PAIR = 2 * P_SIZE
WT = 2 * N + 128
SMALL = 2 * N + HP
NOTE_WIDTH = 16
LOW = jnp.bfloat16
F32 = jnp.float32
NORMAL = (((1,), (0,)), ((), ()))
ROWS_COLS = (((0,), (0,)), ((), ()))
COLS_COLS = (((1,), (1,)), ((), ()))


def mm(a, b, dims=(((1,), (0,)), ((), ()))):
    return lax.dot_general(a.astype(LOW), b.astype(LOW), dims, preferred_element_type=F32)


def exact_mm(a, b, dims=(((1,), (0,)), ((), ()))):
    return lax.dot_general(a, b, dims, precision=HIGHEST, preferred_element_type=F32)


def sibling(x):
    return lax.ppermute(x, "seq", [(0, 1), (1, 0)])


def both_halves(x):
    other = sibling(x)
    first = lax.axis_index("seq") == 0
    return jnp.concatenate([jnp.where(first, x, other), jnp.where(first, other, x)], axis=0)


def own_half(x):
    half = x.shape[0] // 2
    first = lax.axis_index("seq") == 0
    low, high = x[:half], x[half:]
    return jnp.where(first, low, high) + sibling(jnp.where(first, high, low))


def planes_of(x, axis):
    shape = x.shape
    width = shape[axis] // H
    split = x.reshape(shape[:axis] + (HP, PLANES, width) + shape[axis + 1 :])
    return [
        lax.index_in_dim(split, p, axis + 1, keepdims=False).reshape(
            shape[:axis] + (HP * width,) + shape[axis + 1 :]
        )
        for p in range(PLANES)
    ]


def interleave(even, odd, axis):
    shape = even.shape
    width = shape[axis] // HP
    parts = [
        v.reshape(shape[:axis] + (HP, 1, width) + shape[axis + 1 :]) for v in (even, odd)
    ]
    return jnp.concatenate(parts, axis=axis + 1).reshape(
        shape[:axis] + (H * width,) + shape[axis + 1 :]
    )


def adamw(weight, gradient, first_moment, second_moment):
    first_new = BETA_FIRST * first_moment + (1.0 - BETA_FIRST) * gradient
    second_new = BETA_SECOND * second_moment + (1.0 - BETA_SECOND) * gradient * gradient
    first_hat = first_new / (1.0 - BETA_FIRST**STEP)
    second_hat = second_new / (1.0 - BETA_SECOND**STEP)
    weight_new = weight - LEARNING_RATE * (
        first_hat / (jnp.sqrt(second_hat) + ADAM_EPS) + WEIGHT_DECAY * weight
    )
    return (weight_new, first_new, second_new)


def sigmoid(v):
    return 1.0 / (1.0 + jnp.exp(-v))


def softplus(v):
    return jnp.maximum(v, 0.0) + jnp.log1p(jnp.exp(-jnp.abs(v)))


def lower_ones(length):
    row = lax.broadcasted_iota(jnp.int32, (length, length), 0)
    col = lax.broadcasted_iota(jnp.int32, (length, length), 1)
    return (row >= col).astype(F32)


def column(values, index):
    return values[:, index : index + 1]


def per_pair(values, pair, lanes_low):
    return jnp.where(lanes_low, column(values, 2 * pair), column(values, 2 * pair + 1))


def steps_of(dt_raw, heads):
    raw = dt_raw + heads[1:2, :]
    timestep = softplus(raw)
    decay = -jnp.exp(heads[0:1, :]) * timestep
    return raw, timestep, decay


def block_sums(decay):
    ones = lower_ones(BLOCK)
    columns, rows = [], []
    for b in range(decay.shape[0] // BLOCK):
        part = decay[b * BLOCK : (b + 1) * BLOCK]
        columns.append(exact_mm(ones, part))
        rows.append(exact_mm(part, ones, (((0,), (1,)), ((), ()))))
    return columns, rows


def visible_in(seg_col, seg_row, b):
    span = slice(b * BLOCK, (b + 1) * BLOCK)
    row = lax.broadcasted_iota(jnp.int32, (BLOCK, BLOCK), 0)
    col = lax.broadcasted_iota(jnp.int32, (BLOCK, BLOCK), 1)
    return (seg_col[span] == seg_row[:, span]) & (row >= col)


def across(seg_col, seg_row, b):
    return seg_col[b * BLOCK : (b + 1) * BLOCK] == seg_row[:, (b - 1) * BLOCK : b * BLOCK]


def source_of(px_ref, pt_ref, lanes):
    if lanes.start < IP:
        return px_ref[:, lanes]
    return pt_ref[:, lanes.start - IP : lanes.stop - IP]


def forward_kernel(px_ref, pt_ref, taps_ref, heads_ref, segc_ref, segr_ref, mask_ref, pre_ref, y_ref):
    tokens = px_ref.shape[0]
    blocks = tokens // BLOCK
    heads = heads_ref[...]
    seg_col, seg_row = segc_ref[...], segr_ref[...]
    mask = mask_ref[...]
    taps = taps_ref[...]

    def convolve(lanes):
        source = source_of(px_ref, pt_ref, lanes)
        total = taps[CK : CK + 1, lanes] + taps[CK - 1 : CK, lanes] * source
        for back in range(1, CK):
            moved = pltpu.roll(source, back, 0) * column(mask, back)
            total = total + taps[CK - 1 - back : CK - back, lanes] * moved
        pre_ref[:, lanes] = total
        return total * sigmoid(total)

    write_rows = convolve(slice(IP, IP + N))
    read_rows = convolve(slice(IP + N, CP))
    _, timestep, decay = steps_of(pt_ref[:, 2 * N : SMALL], heads)
    sums_col, sums_row = block_sums(decay)
    affinity, crossing = [], [None]
    for b in range(blocks):
        span = slice(b * BLOCK, (b + 1) * BLOCK)
        affinity.append(mm(read_rows[span], write_rows[span], COLS_COLS))
        if b:
            before = slice((b - 1) * BLOCK, b * BLOCK)
            crossing.append(
                jnp.where(
                    across(seg_col, seg_row, b), mm(read_rows[span], write_rows[before], COLS_COLS), 0.0
                ).astype(LOW)
            )
    seen = [visible_in(seg_col, seg_row, b) for b in range(blocks)]
    lanes_low = lax.broadcasted_iota(jnp.int32, (1, PAIR), 1) < P_SIZE
    entry = [jnp.exp(c) for c in sums_col]
    tail = [jnp.exp(c[BLOCK - 1 : BLOCK, :] - c) for c in sums_col]
    for pair in range(HP // 2):
        lanes = slice(pair * PAIR, (pair + 1) * PAIR)
        inputs = convolve(lanes)
        scaled = inputs * per_pair(timestep, pair, lanes_low)
        skip = jnp.where(lanes_low, heads[2:3, 2 * pair : 2 * pair + 1], heads[2:3, 2 * pair + 1 : 2 * pair + 2])
        for b in range(blocks):
            span = slice(b * BLOCK, (b + 1) * BLOCK)
            scores = []
            for h in (2 * pair, 2 * pair + 1):
                spread = column(sums_col[b], h) - sums_row[b][h : h + 1, :]
                scores.append((affinity[b] * jnp.exp(jnp.where(seen[b], spread, MASKED))).astype(LOW))
            here = scaled[span]
            stacked = jnp.concatenate(
                [jnp.where(lanes_low, here, 0.0), jnp.where(lanes_low, 0.0, here)], axis=0
            )
            out = mm(jnp.concatenate(scores, axis=1), stacked)
            if b:
                before = slice((b - 1) * BLOCK, b * BLOCK)
                weighted = scaled[before] * per_pair(tail[b - 1], pair, lanes_low)
                out = out + per_pair(entry[b], pair, lanes_low) * mm(crossing[b], weighted)
            y_ref[span, lanes] = out + skip * inputs[span]


def backward_kernel(
    px_ref,
    pt_ref,
    pre_ref,
    y_ref,
    dy_ref,
    taps_ref,
    heads_ref,
    segc_ref,
    segr_ref,
    mask_ref,
    dx_ref,
    dt_ref,
    dtaps_ref,
    dheads_ref,
):
    tokens = px_ref.shape[0]
    blocks = tokens // BLOCK
    heads = heads_ref[...]
    seg_col, seg_row = segc_ref[...], segr_ref[...]
    mask = mask_ref[...]
    taps = taps_ref[...]

    def activate(lanes):
        pre = pre_ref[:, lanes]
        sig = sigmoid(pre)
        return pre * sig, sig * (1.0 + pre * (1.0 - sig))

    def unconvolve(lanes, grad):
        source = source_of(px_ref, pt_ref, lanes)
        result = taps[CK - 1 : CK, lanes] * grad
        dtaps_ref[CK : CK + 1, lanes] = jnp.sum(grad, axis=0, keepdims=True)
        dtaps_ref[CK - 1 : CK, lanes] = jnp.sum(grad * source, axis=0, keepdims=True)
        for back in range(1, CK):
            at = CK - 1 - back
            kept = grad * column(mask, back)
            moved = pltpu.roll(kept, tokens - back, 0)
            dtaps_ref[at : at + 1, lanes] = jnp.sum(moved * source, axis=0, keepdims=True)
            result = result + taps[at : at + 1, lanes] * moved
        if lanes.start < IP:
            dx_ref[:, lanes] = result.astype(LOW)
        else:
            dt_ref[:, lanes.start - IP : lanes.stop - IP] = result.astype(LOW)

    write_rows, write_slope = activate(slice(IP, IP + N))
    read_rows, read_slope = activate(slice(IP + N, CP))
    raw, timestep, decay = steps_of(pt_ref[:, 2 * N : SMALL], heads)
    sums_col, sums_row = block_sums(decay)
    affinity, crossing = [], [None]
    for b in range(blocks):
        span = slice(b * BLOCK, (b + 1) * BLOCK)
        affinity.append(mm(read_rows[span], write_rows[span], COLS_COLS))
        if b:
            before = slice((b - 1) * BLOCK, b * BLOCK)
            crossing.append(
                jnp.where(
                    across(seg_col, seg_row, b), mm(read_rows[span], write_rows[before], COLS_COLS), 0.0
                ).astype(LOW)
            )
    seen = [visible_in(seg_col, seg_row, b) for b in range(blocks)]
    lanes_low = lax.broadcasted_iota(jnp.int32, (1, PAIR), 1) < P_SIZE
    head_lane = lax.broadcasted_iota(jnp.int32, (1, HP), 1)
    entry = [jnp.exp(c) for c in sums_col]
    tail = [jnp.exp(c[BLOCK - 1 : BLOCK, :] - c) for c in sums_col]
    d_affinity = [jnp.zeros((BLOCK, BLOCK), F32) for _ in range(blocks)]
    d_crossing = [jnp.zeros((BLOCK, BLOCK), F32) for _ in range(blocks)]
    d_sums = [jnp.zeros((BLOCK, HP), F32) for _ in range(blocks)]
    d_steps = [jnp.zeros((BLOCK, HP), F32) for _ in range(blocks)]
    d_skip = jnp.zeros((1, HP), F32)

    def spread_heads(values, pair):
        low = jnp.sum(jnp.where(lanes_low, values, 0.0), axis=1, keepdims=True)
        high = jnp.sum(jnp.where(lanes_low, 0.0, values), axis=1, keepdims=True)
        return jnp.where(head_lane == 2 * pair, low, 0.0) + jnp.where(
            head_lane == 2 * pair + 1, high, 0.0
        )

    for pair in range(HP // 2):
        lanes = slice(pair * PAIR, (pair + 1) * PAIR)
        inputs, slope = activate(lanes)
        step = per_pair(timestep, pair, lanes_low)
        scaled = inputs * step
        skip = jnp.where(lanes_low, heads[2:3, 2 * pair : 2 * pair + 1], heads[2:3, 2 * pair + 1 : 2 * pair + 2])
        y = y_ref[:, lanes]
        d_y = dy_ref[:, lanes]
        d_skip = d_skip + jnp.sum(spread_heads(d_y * inputs, pair), axis=0, keepdims=True)
        d_y_low = d_y.astype(LOW)
        d_y_round = d_y_low.astype(F32)
        scan = y - skip * inputs
        scaled_low = scaled.astype(LOW)
        scaled_round = scaled_low.astype(F32)
        d_scaled = [None] * blocks
        for b in range(blocks):
            span = slice(b * BLOCK, (b + 1) * BLOCK)
            grads, here = d_y_round[span], scaled_low[span]
            stacked = jnp.concatenate(
                [jnp.where(lanes_low, grads, 0.0), jnp.where(lanes_low, 0.0, grads)], axis=0
            ).astype(LOW)
            d_scores = mm(stacked, here, COLS_COLS)
            scores = []
            for i, h in enumerate((2 * pair, 2 * pair + 1)):
                spread = column(sums_col[b], h) - sums_row[b][h : h + 1, :]
                fade = jnp.exp(jnp.where(seen[b], spread, MASKED))
                d_affinity[b] = d_affinity[b] + d_scores[i * BLOCK : (i + 1) * BLOCK] * fade
                scores.append((affinity[b] * fade).astype(LOW))
            d_here = mm(jnp.concatenate(scores, axis=0), stacked, ROWS_COLS)
            d_scaled[b] = d_here if d_scaled[b] is None else d_scaled[b] + d_here
            d_sums[b] = d_sums[b] + spread_heads(grads * scan[span], pair)
            if b:
                before = slice((b - 1) * BLOCK, b * BLOCK)
                tail_here = per_pair(tail[b - 1], pair, lanes_low)
                weighted = (scaled[before] * tail_here).astype(LOW)
                incoming = (d_y[span] * per_pair(entry[b], pair, lanes_low)).astype(LOW)
                d_weighted = mm(crossing[b], incoming, ROWS_COLS)
                d_crossing[b] = d_crossing[b] + mm(incoming, weighted, COLS_COLS)
                d_scaled[b - 1] = d_scaled[b - 1] + tail_here * d_weighted
        for b in range(blocks):
            span = slice(b * BLOCK, (b + 1) * BLOCK)
            d_sums[b] = d_sums[b] - spread_heads(scaled_round[span] * d_scaled[b], pair)
            d_steps[b] = d_steps[b] + spread_heads(inputs[span] * d_scaled[b], pair)
        d_inputs = jnp.concatenate(d_scaled, axis=0) * step + skip * d_y
        unconvolve(lanes, d_inputs * slope)

    ones = lower_ones(BLOCK)
    d_write = [jnp.zeros((BLOCK, N), F32) for _ in range(blocks)]
    d_read = [None] * blocks
    d_decay = [None] * blocks
    later = jnp.zeros((1, HP), F32)
    for b in range(blocks):
        span = slice(b * BLOCK, (b + 1) * BLOCK)
        d_read[b] = mm(d_affinity[b], write_rows[span])
        d_write[b] = d_write[b] + mm(d_affinity[b], read_rows[span], ROWS_COLS)
        if b:
            before = slice((b - 1) * BLOCK, b * BLOCK)
            kept = jnp.where(across(seg_col, seg_row, b), d_crossing[b], 0.0)
            d_read[b] = d_read[b] + mm(kept, write_rows[before])
            d_write[b - 1] = d_write[b - 1] + mm(kept, read_rows[span], ROWS_COLS)
    for b in reversed(range(blocks)):
        d_decay[b] = exact_mm(ones, d_sums[b], ROWS_COLS) + later
        later = later + jnp.sum(d_sums[b], axis=0, keepdims=True)
    unconvolve(slice(IP, IP + N), jnp.concatenate(d_write, axis=0) * write_slope)
    unconvolve(slice(IP + N, CP), jnp.concatenate(d_read, axis=0) * read_slope)
    d_decay = jnp.concatenate(d_decay, axis=0)
    d_raw = (jnp.concatenate(d_steps, axis=0) - d_decay * jnp.exp(heads[0:1, :])) * sigmoid(raw)
    padding = jnp.zeros((tokens, WT - SMALL), LOW)
    dt_ref[:, 2 * N :] = jnp.concatenate([d_raw.astype(LOW), padding], axis=1)
    dheads_ref[0:1, :] = jnp.sum(d_decay * decay, axis=0, keepdims=True)
    dheads_ref[1:2, :] = jnp.sum(d_raw, axis=0, keepdims=True)
    dheads_ref[2:3, :] = d_skip


def call(kernel, outs, *args):
    return pl.pallas_call(
        kernel,
        out_shape=[jax.ShapeDtypeStruct(shape, kind) for shape, kind in outs],
        interpret=INTERPRET,
    )(*args)


def swap(x, by):
    return lax.ppermute(x, "dp", [(i, i ^ by) for i in range(lax.axis_size("dp"))])


def after(x, *earlier):
    return lax.optimization_barrier((x,) + earlier)[0]


def place_kernel(dims, count, at_ref, *refs):
    left_ref = None
    if dims is not None:
        left_ref, refs = refs[0], refs[1:]
    sources, outs = refs[:8], refs[8 : 8 + count]
    chip = at_ref[0]
    rows = sources[0].shape[0] // 2
    for n, source in enumerate(sources):
        for i in range(2):
            k, j = n // 2, n % 2 * 2 + i
            to = pl.multiple_of((chip ^ (4 * j + k)) * rows, rows)
            start = 0
            for out_ref in outs:
                stop = start + out_ref.shape[1]
                out_ref[pl.ds(to, rows), :] = source[i * rows : (i + 1) * rows, start:stop]
                start = stop
    if dims is not None:
        refs[8 + count][...] = mm(left_ref[...], outs[0][...], dims)


def put(sources, left=None, dims=None, widths=None):
    rows = sum(v.shape[0] for v in sources)
    widths = widths or (sources[0].shape[1],)
    outs = [jax.ShapeDtypeStruct((rows, width), LOW) for width in widths]
    extra = []
    if left is not None:
        extra = [left]
        columns = widths[0] if dims[0][1] == (0,) else rows
        outs.append(jax.ShapeDtypeStruct((left.shape[0], columns), F32))
    return pl.pallas_call(
        functools.partial(place_kernel, dims, len(widths)),
        out_shape=outs,
        in_specs=[pl.BlockSpec(memory_space=pltpu.SMEM)] + [pl.BlockSpec()] * (len(extra) + len(sources)),
        interpret=INTERPRET,
    )(lax.axis_index("dp")[None].astype(jnp.int32), *extra, *sources)


def stack_kernel(*refs):
    *sources, top_ref, low_ref = refs
    rows = sources[0].shape[0]
    for n, source in enumerate(sources):
        (top_ref if n < 2 else low_ref)[(n % 2) * rows : (n % 2 + 1) * rows, :] = source[...]


def gather_depth(x, *earlier):
    x = after(x, *earlier) if earlier else x
    return [x] + [swap(x, 4 * j) for j in range(1, 4)]


def gather_plane(parts, *earlier):
    if earlier:
        parts = lax.optimization_barrier(tuple(parts) + earlier)[:4]
    rows, width = parts[0].shape
    top, low = call(stack_kernel, [((2 * rows, width), LOW)] * 2, *parts)
    top_x, top_y, low_x, low_y = swap(top, 1), swap(top, 2), swap(low, 1), swap(low, 2)
    far_top, far_low = swap(top_y, 1), swap(low_x, 2)
    return [top, low, top_x, low_x, top_y, low_y, far_top, far_low]


def add(first, *others):
    total = first.astype(F32)
    for v in others:
        total = total + v.astype(F32)
    return total


def blocks_kernel(at_ref, left_ref, *refs):
    *rights, own_ref, x_ref, y_ref, high_ref, low_ref, whole_ref = refs
    start = 0
    left = left_ref[...]
    for right in rights:
        if right.dtype == LOW:
            width = right.shape[1]
            whole_ref[:, start : start + width] = mm(left, right[...], ROWS_COLS)
            start += width
        else:
            whole_ref[:, start - right.shape[1] : start] += right[...]
    plane = at_ref[0] % 4
    rows = own_ref.shape[1]
    for z in range(4):
        for k, (ref, at) in enumerate(
            ((own_ref, z), (x_ref, z), (y_ref, z), (high_ref if z < 2 else low_ref, z % 2))
        ):
            source = pl.multiple_of((4 * z + (plane ^ k)) * rows, rows)
            ref[at] = whole_ref[pl.ds(source, rows), :].astype(LOW)


def blocks_of(left, *rights):
    rows = left.shape[1] // 16
    width = sum(v.shape[1] for v in rights if v.dtype == LOW)
    return pl.pallas_call(
        blocks_kernel,
        out_shape=[jax.ShapeDtypeStruct((n, rows, width), LOW) for n in (4, 4, 4, 2, 2)],
        in_specs=[pl.BlockSpec(memory_space=pltpu.SMEM)] + [pl.BlockSpec()] * (1 + len(rights)),
        scratch_shapes=[pltpu.VMEM((16 * rows, width), F32)],
        interpret=INTERPRET,
    )(lax.axis_index("dp")[None].astype(jnp.int32), left, *rights)


def scatter_far(blocks):
    return swap(blocks[3], 1), swap(blocks[4], 2)


def near_kernel(x_ref, y_ref, from_x_ref, from_y_ref, *refs):
    *notes, to_x_ref, to_y_ref = refs
    to_x_ref[0:2] = x_ref[0:2]
    to_x_ref[2:4] = (x_ref[2:4].astype(F32) + from_y_ref[...].astype(F32)).astype(LOW)
    to_y_ref[0:2] = (y_ref[0:2].astype(F32) + from_x_ref[...].astype(F32)).astype(LOW)
    to_y_ref[2:4] = y_ref[2:4]
    if notes:
        at = to_y_ref.shape[2] - 128
        lanes = note_lanes(128)
        for z in range(4):
            to_y_ref[z, :, at:] = jnp.where(lanes, notes[0][...], to_y_ref[z, :, at:])


def scatter_near(blocks, arrived, notes=()):
    _, near_x, near_y, _, _ = blocks
    kind = (near_x.shape, LOW)
    to_x, to_y = call(near_kernel, [kind, kind], near_x, near_y, *arrived, *notes)
    return swap(to_x, 1), swap(to_y, 2)


def depth_kernel(at_ref, own_ref, from_x_ref, from_y_ref, *refs):
    *notes, layer_ref, one_ref, two_ref, three_ref = refs
    depth = at_ref[0] // 4
    for j, ref in enumerate((layer_ref, one_ref, two_ref, three_ref)):
        z = depth ^ j
        total = own_ref[z].astype(F32) + from_x_ref[z].astype(F32) + from_y_ref[z].astype(F32)
        ref[...] = total.astype(ref.dtype)
        if notes:
            at = ref.shape[1] - 128
            ref[:, at:] = jnp.where(note_lanes(128), notes[0][...].astype(ref.dtype), ref[:, at:])


def scatter_depth(blocks, arrived, notes=()):
    _, rows, width = blocks[0].shape
    own, *layers = pl.pallas_call(
        depth_kernel,
        out_shape=[jax.ShapeDtypeStruct((rows, width), kind) for kind in (F32, LOW, LOW, LOW)],
        in_specs=[pl.BlockSpec(memory_space=pltpu.SMEM)] + [pl.BlockSpec()] * (3 + len(notes)),
        interpret=INTERPRET,
    )(lax.axis_index("dp")[None].astype(jnp.int32), blocks[0], *arrived, *notes)
    return (own,) + tuple(swap(v, 4 * (j + 1)) for j, v in enumerate(layers))


def note_lanes(width):
    lane = lax.broadcasted_iota(jnp.int32, (1, width), 1)
    return lane >= width - NOTE_WIDTH


def write_notes(values, rows):
    parts, rest = [], values
    for _ in range(3):
        part = lax.reduce_precision(rest, 8, 7)
        parts.append(part)
        rest = rest - part
    tile = jnp.concatenate(parts, axis=0).astype(LOW)
    return jnp.pad(tile, ((0, rows - tile.shape[0]), (128 - NOTE_WIDTH, 0)))


def read_notes(layer):
    parts = layer[:9, layer.shape[1] - NOTE_WIDTH :].astype(F32)
    return parts[0:3] + parts[3:6] + parts[6:9]


def tail_kernel(place_ref, taps_ref, gate_ref, norm_ref, notes_ref, out_ref, full_ref, rows_ref):
    first = place_ref[0] == 0
    none = jnp.zeros((8, P_SIZE), F32)
    for pair in range(HP // 2):
        v = taps_ref[:, pair * PAIR : (pair + 1) * PAIR]
        a, b = v[:, :P_SIZE], v[:, P_SIZE:]
        even = jnp.concatenate([a, none, b, none], axis=1)
        odd = jnp.concatenate([none, a, none, b], axis=1)
        full_ref[:, pair * 2 * PAIR : (pair + 1) * 2 * PAIR] = jnp.where(first, even, odd)
    full_ref[:, DI:] = taps_ref[:, IP:]
    rows_ref[...] = jnp.zeros(rows_ref.shape, F32)
    rows_ref[0:1, :] = norm_ref[...]
    rows_ref[1:2, :] = gate_ref[...]
    span = rows_ref.shape[1] // 32
    each = CONV // 32
    taps = CK + 1
    for core in range(32):
        for g in range(-(-each // span)):
            width = min(span, each - g * span)
            source = core * each + g * span
            rows_ref[2 + taps * g : 2 + taps * (g + 1), core * span : core * span + width] = full_ref[
                0:taps, source : source + width
            ]
    row = lax.broadcasted_iota(jnp.int32, (32, 128), 0)
    col = lax.broadcasted_iota(jnp.int32, (32, 128), 1)
    columns = mm(rows_ref[...], col == row + HP, ROWS_COLS)
    height = notes_ref.shape[0]
    for block in range(16):
        at = slice(block * height, (block + 1) * height)
        out_ref[at, :] = columns[at, :] + notes_ref[...].astype(F32)


def tail_columns(d_taps, d_gate, d_norm, notes):
    rows = d_norm.shape[1]
    return pl.pallas_call(
        tail_kernel,
        out_shape=jax.ShapeDtypeStruct((rows, 128), F32),
        in_specs=[pl.BlockSpec(memory_space=pltpu.SMEM)] + [pl.BlockSpec()] * 4,
        scratch_shapes=[pltpu.VMEM((8, CONV), F32), pltpu.VMEM((32, rows), F32)],
        interpret=INTERPRET,
    )(lax.axis_index("seq")[None].astype(jnp.int32), d_taps, d_gate, d_norm, notes)


def split_kernel(place_ref, w_ref, tail_ref, mine_ref, other_ref):
    first = place_ref[0] == 0
    shared = w_ref[:, 2 * DI : DI + CONV].astype(LOW)
    for ref, p in ((mine_ref, 0), (other_ref, 1)):
        ref[:, : 2 * N] = shared
        ref[:, 2 * N : WT] = tail_ref[p]
    for group in range(IP // 128):
        for base, to in ((DI, WT), (0, WT + IP)):
            at = base + 256 * group
            block = w_ref[:, at : at + 256]
            even = jnp.concatenate([block[:, 0:64], block[:, 128:192]], axis=1)
            odd = jnp.concatenate([block[:, 64:128], block[:, 192:256]], axis=1)
            lanes = slice(to + 128 * group, to + 128 * (group + 1))
            mine_ref[:, lanes] = jnp.where(first, even, odd).astype(LOW)
            other_ref[:, lanes] = jnp.where(first, odd, even).astype(LOW)


def small_width(rows):
    per_core = CONV // (DI // P_SIZE)
    return per_core * (CK + 1), -(-(per_core * (CK + 1)) // rows)


def payloads(norm_gain, in_weight, conv_weight, gate_gain):
    place = lax.axis_index("seq")
    first = place == 0
    rows = in_weight.shape[0]
    values, width = small_width(rows)
    steps = planes_of(in_weight[:, DI + CONV :], 1)
    conv_flat = jnp.pad(conv_weight.reshape(-1), (0, rows * width - values)).reshape(rows, width)
    gate_two = gate_gain.reshape(2, rows).T
    zero = jnp.zeros_like(gate_two)
    fill = jnp.zeros((rows, WT - SMALL - 3 - width), F32)

    def tail(step, gate):
        return jnp.concatenate([step, norm_gain[:, None], gate, conv_flat, fill], axis=1)

    tails = jnp.stack(
        [
            tail(jnp.where(first, steps[0], steps[1]), gate_two),
            tail(jnp.where(first, steps[1], steps[0]), zero),
        ]
    ).astype(LOW)
    shape = jax.ShapeDtypeStruct((rows, WT + 2 * IP), LOW)
    mine, send = pl.pallas_call(
        split_kernel,
        out_shape=[shape, shape],
        in_specs=[pl.BlockSpec(memory_space=pltpu.SMEM), pl.BlockSpec(), pl.BlockSpec()],
        interpret=INTERPRET,
    )(place[None].astype(jnp.int32), in_weight, tails)
    other = sibling(send)
    chip = jnp.concatenate([jnp.where(first, mine, other), jnp.where(first, other, mine)], axis=0)
    return chip[:, : WT + IP], chip[:, WT + IP :]


def unpack(w_t):
    chips = 16
    rows = w_t.shape[0] // (2 * chips)
    values, width = small_width(rows)
    small = w_t[:, SMALL : SMALL + 3 + width].astype(F32)
    norm = small[:, 0]
    gate = small[:, 1:3].reshape(chips, 2, rows, 2).sum(1).transpose(0, 2, 1).reshape(-1)
    conv = small[:, 3:].reshape(2 * chips, rows * width)[:, :values].reshape(CONV, CK + 1).T
    return norm, gate, plane_taps(conv)


def plane_taps(conv):
    x = planes_of(conv[:, :DI], 1)
    x = jnp.where(lax.axis_index("seq") == 0, x[0], x[1])
    taps = jnp.concatenate([x, conv[:, DI:]], axis=1)
    return jnp.pad(taps, ((0, 8 - taps.shape[0]), (0, 0)))


def all_taps(d_taps):
    d_taps = d_taps[: CK + 1]
    x, shared = d_taps[:, :IP], d_taps[:, IP:]
    first = lax.axis_index("seq") == 0
    none = jnp.zeros_like(x)
    even, odd = jnp.where(first, x, none), jnp.where(first, none, x)
    return jnp.concatenate([interleave(even, odd, 1), shared], axis=1).T


def all_heads(d_heads):
    first = lax.axis_index("seq") == 0
    none = jnp.zeros_like(d_heads)
    return interleave(jnp.where(first, d_heads, none), jnp.where(first, none, d_heads), 1)


def rows_back(chip_rows):
    first = lax.axis_index("seq") == 0
    rows = chip_rows.shape[0] // 2
    low, high = chip_rows[:rows], chip_rows[rows:]
    keep = jnp.where(first, low, high)
    other = sibling(jnp.where(first, high, low))
    return jnp.where(first, keep, other), jnp.where(first, other, keep)


def update_kernel(
    z_even, z_odd, a_even, a_odd, weight, first, second, grad_ref, weight_ref, first_ref, second_ref
):
    def update(at, grad):
        lanes = slice(at, at + grad.shape[1])
        grad_ref[:, lanes] = grad
        new = adamw(weight[:, lanes], grad, first[:, lanes], second[:, lanes])
        weight_ref[:, lanes], first_ref[:, lanes], second_ref[:, lanes] = new

    for base, even, odd in ((0, z_even, z_odd), (DI, a_even, a_odd)):
        for group in range(IP // 128):
            e = even[:, 128 * group : 128 * (group + 1)]
            o = odd[:, 128 * group : 128 * (group + 1)]
            pieces = [e[:, :P_SIZE], o[:, :P_SIZE], e[:, P_SIZE:], o[:, P_SIZE:]]
            update(base + 256 * group, jnp.concatenate(pieces, axis=1))
    shared = slice(IP, IP + 2 * N)
    update(2 * DI, a_even[:, shared] + a_odd[:, shared])
    at = IP + 2 * N
    e, o = a_even[:, at : at + 128], a_odd[:, at : at + 128]
    row = lax.broadcasted_iota(jnp.int32, (128, H), 0)
    col = lax.broadcasted_iota(jnp.int32, (128, H), 1)
    update(DI + CONV, exact_mm(e, (col == 2 * row).astype(F32)) + exact_mm(o, (col == 2 * row + 1).astype(F32)))


def fetch_any(norm_low, in_low, conv_low, gate_low, out_low):
    norm, w_in, conv, gate, w_out = (
        lax.all_gather(v, ("dp", "seq"), axis=0, tiled=True)
        for v in (norm_low, in_low, conv_low, gate_low, out_low)
    )
    first = lax.axis_index("seq") == 0

    def mine(v, axis):
        parts = planes_of(v, axis)
        return jnp.where(first, parts[0], parts[1])

    w_t = jnp.concatenate(
        [
            w_in[:, 2 * DI : DI + CONV],
            mine(w_in[:, DI + CONV :], 1),
            jnp.zeros((w_in.shape[0], WT - SMALL), LOW),
        ],
        axis=1,
    )
    return (
        w_t,
        mine(w_in[:, DI : 2 * DI], 1),
        mine(w_in[:, :DI], 1),
        mine(w_out, 0),
        norm.astype(F32),
        mine(gate, 0).astype(F32),
        plane_taps(conv.astype(F32).T),
    )


def embed(v, axis):
    first = lax.axis_index("seq") == 0
    none = jnp.zeros_like(v)
    return interleave(jnp.where(first, v, none), jnp.where(first, none, v), axis)


def return_any(d_t, d_x, d_z, d_norm, d_gate, d_taps, d_out):
    def total(v):
        return lax.psum_scatter(v, ("dp", "seq"), scatter_dimension=0, tiled=True)

    d_in = jnp.concatenate(
        [embed(d_z, 1), embed(d_x, 1), d_t[:, : 2 * N], embed(d_t[:, 2 * N : SMALL], 1)], axis=1
    )
    return (
        total(d_in.astype(LOW)).astype(F32),
        total(d_norm),
        total(all_taps(d_taps)),
        total(embed(d_gate, 0)),
        total(embed(d_out, 0).astype(LOW)).astype(F32),
    )


def on_device(
    resid,
    segment_ids,
    cotangent,
    norm_gain,
    in_weight,
    conv_weight,
    gate_gain,
    out_weight,
    head_params,
    first_norm,
    first_in,
    first_conv,
    first_gate,
    first_out,
    first_head,
    second_norm,
    second_in,
    second_conv,
    second_gate,
    second_out,
    second_head,
):
    place = lax.axis_index("seq")
    local_rows = resid[0]
    cot_rows = cotangent[0]
    segments = segment_ids[0]
    tokens = segments.shape[0]
    one_head = out_weight.shape[0] == P_SIZE and lax.axis_size("dp") == 16
    all_rows = both_halves(local_rows)
    cot_half = both_halves(cot_rows.astype(LOW))

    def inverse_rms(values):
        return lax.rsqrt(jnp.mean(values * values, axis=-1, keepdims=True) + NORM_EPS)

    if one_head:
        low_a, low_z = payloads(norm_gain, in_weight, conv_weight, gate_gain)
        deep_a = gather_depth(low_a)
        segments, head_params_here = lax.optimization_barrier((segments, head_params) + tuple(deep_a[1:]))[:2]
    else:
        head_params_here = head_params
    heads = planes_of(head_params_here, 1)
    heads = jnp.pad(jnp.where(place == 0, heads[0], heads[1]), ((0, 5), (0, 0)))
    seg_col, seg_row = segments[:, None], segments[None, :]
    masks = [jnp.ones((tokens,), F32)]
    for back in range(1, CK):
        same = (segments[back:] == segments[:-back]).astype(F32)
        masks.append(jnp.concatenate([jnp.zeros((back,), F32), same]))
    mask = jnp.stack(masks, axis=1)

    def normed_by(norm):
        return (all_rows * inverse_rms(all_rows) * norm).astype(LOW)

    if one_head:
        parts_a = gather_plane(deep_a)
        deep_z = gather_depth(low_z, *deep_a[1:])
        parts_z = gather_plane(deep_z, *parts_a[2:6])
        deep_out = gather_depth(out_weight.astype(LOW), *deep_z[1:])
        parts_out = gather_plane(deep_out, *parts_z[2:6])
        *parts_a, cot_half = lax.optimization_barrier((*parts_a, cot_half))
        w_t, w_x = put(parts_a, widths=(WT, IP))
        norm, gate, taps = unpack(w_t)
        normed_half = normed_by(norm)
        proj_t = mm(normed_half, w_t)
        proj_x = mm(normed_half, w_x)
        w_z, z = put(parts_z, normed_half, NORMAL)
        w_out, grad_mixed = put(parts_out, cot_half, COLS_COLS)
    else:
        lows = [v.astype(LOW) for v in (norm_gain, in_weight, conv_weight, gate_gain, out_weight)]
        w_t, w_x, w_z, w_out, norm, gate, taps = fetch_any(*lows)
        normed_half = normed_by(norm)
        proj_t, proj_x, z = (mm(normed_half, w) for w in (w_t, w_x, w_z))
        grad_mixed = mm(cot_half, w_out, COLS_COLS)
    pre, y = call(
        forward_kernel,
        [((tokens, CP), F32), ((tokens, IP), F32)],
        proj_x,
        proj_t,
        taps,
        heads,
        seg_col,
        seg_row,
        mask,
    )
    sig = sigmoid(z)
    silu = z * sig
    gated = y * silu
    partial = jnp.stack(
        [jnp.sum(gated * gated, axis=1), jnp.sum(grad_mixed * gate * gated, axis=1)], axis=0
    )
    both = partial + sibling(partial)
    scale = lax.rsqrt(both[0] / DI + NORM_EPS)
    pull = (scale * scale * scale * both[1] / DI)[:, None]
    scale = scale[:, None]
    mixed_half = (gated * scale * gate).astype(LOW)
    if one_head:
        blocks_out = blocks_of(mixed_half, cot_half)
        far_out = scatter_far(blocks_out)
        scale = after(scale, *blocks_out[3:])
    d_gated = scale * (grad_mixed * gate) - gated * pull
    d_z = (d_gated * y * (sig * (1.0 + z * (1.0 - sig)))).astype(LOW)
    d_y = d_gated * silu
    d_gate = jnp.sum(grad_mixed * gated * scale, axis=0)
    if one_head:
        blocks_z = blocks_of(normed_half, d_z)
        far_z = scatter_far(blocks_z)
        near_out = scatter_near(blocks_out, far_out)
        near_z = scatter_near(blocks_z, far_z)
        d_y = after(d_y, *far_out, *far_z)
    d_proj_x, d_proj_t, d_taps, d_heads = call(
        backward_kernel,
        [((tokens, IP), LOW), ((tokens, WT), LOW), ((8, CP), F32), ((3, HP), F32)],
        proj_x,
        proj_t,
        pre,
        y,
        d_y,
        taps,
        heads,
        seg_col,
        seg_row,
        mask,
    )
    partial_normed = mm(d_proj_x, w_x, COLS_COLS) + mm(d_proj_t, w_t, COLS_COLS) + mm(d_z, w_z, COLS_COLS)
    d_norm = jnp.sum(partial_normed * all_rows * inverse_rms(all_rows), axis=0)
    if one_head:
        rows = in_weight.shape[0]
        notes = write_notes(d_heads, 2 * rows)
        small = tail_columns(d_taps, d_gate[None], d_norm[None], notes)
        blocks_a = blocks_of(normed_half, d_proj_x, d_proj_t, small)
        far_a = scatter_far(blocks_a)
        terms_out = scatter_depth(blocks_out, near_out)
        heads_here = read_notes(notes) + read_notes(far_a[0][0])
        notes = write_notes(heads_here, 2 * rows)
        near_a = scatter_near(blocks_a, far_a, (notes,))
        terms_z = scatter_depth(blocks_z, near_z)
        heads_here = read_notes(notes) + read_notes(near_a[1][0])
        terms_a = scatter_depth(blocks_a, near_a, (write_notes(heads_here, 2 * rows),))
        partial_normed, mixed_half, *terms = lax.optimization_barrier(
            (partial_normed, mixed_half) + terms_out[1:] + terms_z[1:] + terms_a[:1]
        )[:8]
        shard_out = add(terms_out[0], *terms[:3])
        back_z = rows_back(add(terms_z[0], *terms[3:]))
    else:
        d_in_t, d_in_x, d_in_z = (mm(normed_half, v, ROWS_COLS) for v in (d_proj_t, d_proj_x, d_z))
        d_out = mm(mixed_half, cot_half, ROWS_COLS)
        shard_in, shard_norm, shard_conv, shard_gate, shard_out = return_any(
            d_in_t, d_in_x, d_in_z, d_norm, d_gate, d_taps, d_out
        )
        head_total = lax.psum(all_heads(d_heads), ("dp", "seq"))

    other_half = own_half(mm(mixed_half, w_out))
    grad_normed = own_half(partial_normed)
    result = local_rows + other_half
    inv = inverse_rms(local_rows)
    weighted = grad_normed * norm
    dots = jnp.mean(weighted * local_rows, axis=-1, keepdims=True)
    grad_input = cot_rows + inv * weighted - local_rows * (inv * inv * inv * dots)
    updated_out = adamw(out_weight, shard_out, first_out, second_out)
    if one_head:
        early = (result, grad_input, shard_out, *updated_out, *back_z)
        late = lax.optimization_barrier(early + terms_a)
        result, grad_input, shard_out, *updated_out = late[:6]
        back_z, terms_a = late[6:8], late[8:]
        chip_a = add(*terms_a)
        depth = lax.axis_index("dp") // 4
        every = jnp.stack([read_notes(v) for v in terms_a])
        every = [lax.dynamic_index_in_dim(every, depth ^ j, 0, keepdims=False) for j in range(4)]
        d_heads = every[0] + every[1] + every[2] + every[3]
        other = sibling(d_heads)
        first = place == 0
        head_total = interleave(jnp.where(first, d_heads, other), jnp.where(first, other, d_heads), 1)
        back_a = rows_back(chip_a)
        tail = back_a[0][:, IP + 2 * N :] + back_a[1][:, IP + 2 * N :]
        shape = (in_weight.shape, F32)
        new_in = call(update_kernel, [shape] * 4, *back_z, *back_a, in_weight, first_in, second_in)
        shard_in = new_in[0]
        small = tail[:, HP:]
        shard_norm = small[:, 0]
        shard_gate = chip_a[:, IP + SMALL + 1]
        groups = -(-conv_weight.shape[0] // rows)
        conv = small[:, 2 : 2 + groups * (CK + 1)].reshape(rows, groups, CK + 1).transpose(1, 0, 2)
        shard_conv = conv.reshape(-1, CK + 1)[: conv_weight.shape[0]]
        updated_in = new_in[1:]
    else:
        updated_in = adamw(in_weight, shard_in, first_in, second_in)
    new_norm, new_first_norm, new_second_norm = adamw(
        norm_gain, shard_norm, first_norm, second_norm
    )
    new_in, new_first_in, new_second_in = updated_in
    new_conv, new_first_conv, new_second_conv = adamw(
        conv_weight, shard_conv, first_conv, second_conv
    )
    new_gate, new_first_gate, new_second_gate = adamw(
        gate_gain, shard_gate, first_gate, second_gate
    )
    new_out, new_first_out, new_second_out = updated_out
    new_head, new_first_head, new_second_head = adamw(
        head_params, head_total, first_head, second_head
    )
    return (
        result[None],
        grad_input[None],
        shard_norm,
        shard_in,
        shard_conv,
        shard_gate,
        shard_out,
        head_total,
        new_norm,
        new_in,
        new_conv,
        new_gate,
        new_out,
        new_head,
        new_first_norm,
        new_first_in,
        new_first_conv,
        new_first_gate,
        new_first_out,
        new_first_head,
        new_second_norm,
        new_second_in,
        new_second_conv,
        new_second_gate,
        new_second_out,
        new_second_head,
    )


def solution(mesh):
    step = whole_step(mesh)
    return step


def whole_step(mesh):
    rows = P(("dp", "seq"))
    wide = P(("dp", "seq"), None)
    tokens = P("dp", "seq", None)
    weights = (rows, wide, wide, rows, wide, P())

    return jax.shard_map(
        on_device,
        mesh=mesh,
        in_specs=(tokens, P("dp", None), tokens) + weights * 3,
        out_specs=(tokens, tokens) + weights_out() * 4,
        check_vma=False,
    )


def weights_out():
    rows = P(("dp", "seq"))
    wide = P(("dp", "seq"), None)
    return (rows, wide, wide, rows, wide, P())
```
